128 devices in a mesh: pipe: 8 (over y, core), expert: 16 (over z, x).
Axes of the slice: x: 4, y: 4, z: 4, core: 2. Of those that a mesh axis runs over, the one named last changes fastest.
Arguments:
- boundary_grad: bfloat16 [8, 4096, 3584], P('pipe', 'expert'), may hold values from -6 to 6
- route_ids: int32 [8, 4096, 8], P('pipe', 'expert'), may hold values from 0 to 255, as said below
- route_probs: bfloat16 [8, 4096, 8], P('pipe', 'expert'), may hold values from 0.049804688 to 1
- saved_preact: bfloat16 [8, 16, 1024, 2048], P('pipe', 'expert'), may hold values from -6 to 6
- down_weight: bfloat16 [8, 16, 1024, 3584], P('pipe', 'expert'), may hold values from -0.046875 to 0.046875
Outputs:
- preact_grad: bfloat16 [8, 16, 1024, 2048], P('pipe', 'expert')
- down_grad: bfloat16 [8, 16, 1024, 3584], P('pipe', 'expert')
- prob_grad: float32 [8, 4096, 8], P('pipe', 'expert')
The draws below stay inside these ranges and needn't reach their ends.
Inputs may be any that keep to these rules, and one draw needn't show every extreme that they name: `route_ids`: each token names 8 different experts. Window experts are 0 to 15. In each aligned block of 256 tokens of a section (the tokens of one device) each window expert is named by at most 64 tokens, and in every section one window expert is named by exactly 64 tokens of every block.
All inputs are finite; a program needn't handle non-finite values.
Results may differ from the reference program's by a relative error of at most 0.0057.
Values may be sent and summed in bfloat16 or wider, within the bound.
A program may use at most 192 MiB of HBM per device.

```python
import jax
import jax.numpy as jnp
from jax import lax

D = 3584
H = 1024
K = 8
ROUTED = 256
TOK_DEV = 256
CAP = 64
SECTIONS = 8
EXPERTS = 16
TOKENS = 4096
SLOTS = 1024


def draw_route_ids(key, part):
    keys = jax.random.split(jax.random.fold_in(key, 17), 4)
    blocks = TOKENS // TOK_DEV
    noise = jax.random.randint(keys[0], (SECTIONS, TOKENS, ROUTED), 0, 1024)
    level = jax.random.randint(keys[1], (SECTIONS, 1, ROUTED), 0, 4)
    expert_id = jnp.arange(ROUTED, dtype=jnp.int32)[None, None, :]
    window = expert_id < EXPERTS
    level = jnp.where(window, level + 2, level)
    base = (noise + level * 512) * ROUTED + expert_id
    shuffle = jax.random.randint(keys[2], (SECTIONS, blocks, TOK_DEV, EXPERTS), 0, 65536)
    shuffle = shuffle * TOK_DEV + jnp.arange(TOK_DEV, dtype=jnp.int32)[None, None, :, None]
    position = jnp.argsort(jnp.argsort(shuffle, axis=2), axis=2)
    allowed = (position < CAP).reshape(SECTIONS, TOKENS, EXPERTS)
    allowed_full = jnp.concatenate([allowed, jnp.ones((SECTIONS, TOKENS, ROUTED - EXPERTS), dtype=bool)], axis=2)
    hottest = jax.random.randint(keys[3], (SECTIONS, 1, 1), 0, EXPERTS)
    score = jnp.where(allowed_full, base, -1)
    score = jnp.where(allowed_full & (expert_id == hottest), base + 2097152, score)
    return lax.top_k(score, K)[1].astype(jnp.int32)


def shard_levels(own_key, shape, cuts, least, largest):
    def one(dim, parts):
        heights = jax.random.uniform(jax.random.fold_in(jax.random.fold_in(own_key, 6), dim), (parts,), jnp.float32, least / len(cuts), largest / len(cuts))
        return jnp.repeat(jnp.exp(heights), shape[dim] // parts).reshape((-1,) + (1,) * (len(shape) - dim - 1))

    level = one(*cuts[0])
    for cut in cuts[1:]:
        level = level * one(*cut)
    return level


def centred(rng, shape, spread, most, shards=(), held_as=jnp.bfloat16):
    gain = shard_levels(rng, shape, shards, -0.22, 0.18) if shards else 1.0
    result = jax.random.normal(rng, shape, jnp.float32) * spread * gain
    return jnp.minimum(jnp.maximum(result, -most), most).astype(held_as)


def setup_inputs(seed: int = 0) -> dict:
    streams_of = jax.random.split(jax.random.key(seed), 6)
    boundary_grad = centred(streams_of[0], (SECTIONS, TOKENS, D), 1.0, 6.0, ((0, 8), (1, 16)))
    route_ids = draw_route_ids(jax.random.fold_in(streams_of[5], 71), 0)
    route_probs = jnp.clip(0.049804688 + 0.9501953 * jax.random.uniform(streams_of[2], (SECTIONS, TOKENS, K), jnp.float32) ** shard_levels(streams_of[2], (SECTIONS, TOKENS, K), ((0, 8), (1, 16)), -0.2, 0.2), 0.049804688, 1.0).astype(jnp.bfloat16)
    saved_preact = centred(streams_of[3], (SECTIONS, EXPERTS, SLOTS, 2 * H), 1.0, 6.0, ((0, 8), (1, 16)))
    down_weight = centred(streams_of[4], (SECTIONS, EXPERTS, H, D), (16 * H) ** -0.5, 0.046875, ((0, 8), (1, 16)))
    return {"boundary_grad": boundary_grad, "route_ids": route_ids, "route_probs": route_probs, "saved_preact": saved_preact, "down_weight": down_weight}


def activation(gate_up):
    half_width = gate_up.shape[1] // 2
    gate_pre = gate_up[:, :half_width].astype(jnp.float32)
    up_pre = gate_up[:, half_width:].astype(jnp.float32)
    sigmoid_gate = jax.nn.sigmoid(gate_pre)
    return gate_pre, up_pre, sigmoid_gate


def expert_backward(gate_up, row_grad, row_prob, weight):
    gate_pre, up_pre, sigmoid_gate = activation(gate_up)
    silu_gate = gate_pre * sigmoid_gate
    hidden = (silu_gate * up_pre).astype(jnp.bfloat16)
    weighted = (row_prob.astype(jnp.float32)[:, None] * row_grad.astype(jnp.float32)).astype(jnp.bfloat16)
    expert_out = jnp.dot(hidden, weight, preferred_element_type=jnp.float32)
    slot_prob = jnp.sum(row_grad.astype(jnp.float32) * expert_out, axis=1)
    hidden_grad = jnp.dot(weighted, weight.T, preferred_element_type=jnp.float32)
    gate_grad = hidden_grad * up_pre * sigmoid_gate * (1.0 + gate_pre * (1.0 - sigmoid_gate))
    up_grad = hidden_grad * silu_gate
    preact = jnp.concatenate([gate_grad, up_grad], axis=1).astype(jnp.bfloat16)
    weight_grad = jnp.dot(hidden.T, weighted, preferred_element_type=jnp.float32)
    return preact, weight_grad.astype(jnp.bfloat16), slot_prob


def reference(boundary_grad, route_ids, route_probs, saved_preact, down_weight):
    blocks = TOKENS // TOK_DEV
    preact_all = []
    weight_all = []
    prob_all = []
    for section in range(SECTIONS):
        out_grad = boundary_grad[(section + 1) % SECTIONS]
        routes = route_ids[section]
        probs = route_probs[section].astype(jnp.float32)

        def one_expert(expert):
            route_hits = routes == expert
            member = jnp.sum(route_hits.astype(jnp.int32), axis=1)
            blocked = member.reshape(blocks, TOK_DEV)
            slot_rank = jnp.cumsum(blocked, axis=1) - 1
            block_base = (jnp.arange(blocks, dtype=jnp.int32) * CAP)[:, None]
            token_slot = jnp.where(blocked == 1, block_base + slot_rank, SLOTS).reshape(TOKENS).astype(jnp.int32)
            slot_token = jnp.zeros((SLOTS + 1,), jnp.int32).at[token_slot].set(jnp.arange(TOKENS, dtype=jnp.int32))[:SLOTS]
            slot_live = jnp.zeros((SLOTS + 1,), jnp.int32).at[token_slot].set(1)[:SLOTS]
            token_prob = jnp.sum(jnp.where(route_hits, probs, 0.0), axis=1)
            row_grad = jnp.where(slot_live[:, None] == 1, out_grad[slot_token], jnp.zeros((), out_grad.dtype))
            row_prob = jnp.where(slot_live == 1, token_prob[slot_token], 0.0)
            preact, weight_grad, slot_prob = expert_backward(saved_preact[section, expert], row_grad, row_prob, down_weight[section, expert])
            padded = jnp.concatenate([slot_prob, jnp.zeros((1,), slot_prob.dtype)])
            token_grad = padded[token_slot]
            prob_term = jnp.where(route_hits, token_grad[:, None], 0.0)
            return preact, weight_grad, prob_term

        preact, weight_grad, prob_term = lax.map(one_expert, jnp.arange(EXPERTS, dtype=jnp.int32))
        preact_all.append(preact)
        weight_all.append(weight_grad)
        prob_all.append(jnp.sum(prob_term, axis=0))
    return jnp.stack(preact_all), jnp.stack(weight_all), jnp.stack(prob_all)
```

```python
import functools

import jax
import jax.numpy as jnp
from jax import lax
from jax.experimental import pallas as pl
from jax.experimental.pallas import tpu as pltpu
from jax.sharding import PartitionSpec as P

MESH = pl.DeviceIdType.MESH
F32 = jnp.float32
BF16 = jnp.bfloat16
COLS = 256
LAG = 5


def exchange_kernel(
    grad_hbm,
    route_ref,
    prob_ref,
    pre_hbm,
    weight_hbm,
    hidden_grad,
    down_grad,
    prob_grad,
    shifted,
    line,
    outgoing,
    rows,
    weight,
    pre,
    hidden,
    scaled_t,
    codes,
    picks,
    own_picks,
    prob_tiles,
    back_tile,
    back_tiles,
    row_prob,
    load_sem,
    shift_send,
    shift_recv,
    own_send,
    forward_send,
    line_recv,
    out_send,
    rows_recv,
    code_send,
    code_recv,
    tile_send,
    tile_recv,
    back_send,
    back_recv,
):
    chunks = shifted.shape[0]
    pipe = lax.axis_index("pipe")
    me = lax.axis_index("expert")
    z, x = me // 4, me % 4
    before = lax.rem(pipe + 7, 8)

    def along_x(step):
        return z * 4 + lax.rem(x + step, 4)

    def along_z(step):
        return lax.rem(z + step, 4) * 4 + x

    def first_axis(half, step):
        return along_x(step) * (1 - half) + along_z(step) * half

    def second_axis(half, step):
        return along_z(step) * (1 - half) + along_x(step) * half

    def remote(src, dst, send, recv, device):
        return pltpu.make_async_remote_copy(
            src_ref=src,
            dst_ref=dst,
            send_sem=send,
            recv_sem=recv,
            device_id=device,
            device_id_type=MESH,
        )

    barrier = pltpu.get_barrier_semaphore()
    for step in range(1, 16):
        pl.semaphore_signal(
            barrier, inc=1, device_id=(pipe, lax.rem(me + step, 16)), device_id_type=MESH
        )
    for step in (1, 7):
        pl.semaphore_signal(
            barrier, inc=1, device_id=(lax.rem(pipe + step, 8), me), device_id_type=MESH
        )

    pre_load = pltpu.make_async_copy(pre_hbm, pre, load_sem.at[chunks])
    pre_load.start()

    def weight_load(c):
        return pltpu.make_async_copy(
            weight_hbm.at[:, pl.ds(pl.multiple_of(c * COLS, COLS), COLS)],
            weight.at[c],
            load_sem.at[c],
        )

    @pl.loop(0, chunks)
    def _(c):
        weight_load(c).start()

    expert_iota = lax.broadcasted_iota(jnp.int32, (16, 256), 0)
    member = jnp.zeros((16, 256), F32)
    token_prob = jnp.zeros((16, 256), F32)
    for k in range(8):
        hit = route_ref[k : k + 1, :] == expert_iota
        member = member + jnp.where(hit, 1.0, 0.0)
        token_prob = token_prob + jnp.where(hit, prob_ref[k : k + 1, :].astype(F32), 0.0)
    earlier = (
        lax.broadcasted_iota(jnp.int32, (256, 256), 0)
        <= lax.broadcasted_iota(jnp.int32, (256, 256), 1)
    )
    rank = jnp.dot(
        member.astype(BF16), jnp.where(earlier, 1.0, 0.0).astype(BF16), preferred_element_type=F32
    )
    codes[0] = jnp.where(member > 0.5, rank - 1.0, -1.0)
    slot_iota = lax.broadcasted_iota(jnp.int32, (64, 256), 0).astype(F32)
    for e in range(16):
        own_picks[e * 64 : e * 64 + 64, :] = jnp.where(
            codes[0, e : e + 1, :] == slot_iota, 1.0, 0.0
        ).astype(BF16)
    diagonal = (
        lax.broadcasted_iota(jnp.int32, (16, 1024), 1) // 64
        == lax.broadcasted_iota(jnp.int32, (16, 1024), 0)
    )
    slot_probs = lax.dot_general(
        token_prob.astype(BF16),
        own_picks[...],
        (((1,), (1,)), ((), ())),
        preferred_element_type=F32,
    )
    slot_probs = jnp.sum(jnp.where(diagonal, slot_probs, 0.0), axis=0, keepdims=True)
    for r in range(8):
        prob_tiles[me, r : r + 1, :] = slot_probs[:, r * 128 : r * 128 + 128]

    pl.semaphore_wait(barrier, 17)

    def shift_copy(c):
        return remote(
            grad_hbm.at[:, pl.ds(pl.multiple_of(c * COLS, COLS), COLS)],
            shifted.at[c],
            shift_send.at[c],
            shift_recv.at[c],
            (before, me),
        )

    @pl.loop(0, chunks)
    def _(c):
        shift_copy(c).start()

    code_copies = []
    for half, towards in ((0, along_x), (1, along_z)):
        for slot, step in ((1, 1), (2, 3), (3, 2)):
            index = half * 3 + slot
            code_copies.append(
                remote(
                    codes.at[0],
                    codes.at[index],
                    code_send.at[index - 1],
                    code_recv.at[index - 1],
                    (pipe, towards(step)),
                )
            )
    for copy in code_copies:
        copy.start()

    def tile_copy(step):
        return remote(
            prob_tiles.at[me],
            prob_tiles.at[me],
            tile_send.at[step],
            tile_recv.at[step],
            (pipe, lax.rem(me + step, 16)),
        )

    @pl.loop(1, 16)
    def _(step):
        tile_copy(step).start()

    def own_copy(c, side):
        half = lax.rem(c, 2)
        return remote(
            shifted.at[c],
            line.at[c, side],
            own_send.at[c, side],
            line_recv.at[c, side],
            (pipe, first_axis(half, 1 if side == 0 else 3)),
        )

    def forward_copy(c, side):
        half = lax.rem(c, 2)
        part = pl.ds(side * 128, 128)
        return remote(
            line.at[c, side, part],
            line.at[c, 2, part],
            forward_send.at[c, side],
            line_recv.at[c, 2 + side],
            (pipe, first_axis(half, 1 if side == 0 else 3)),
        )

    def out_copy(c, step, half):
        target = rows.at[c, z] if half == 0 else rows.at[c, :, x]
        return remote(
            outgoing.at[c, step - 1],
            target,
            out_send.at[c, step - 1],
            rows_recv.at[c, step - 1],
            (pipe, second_axis(half, step)),
        )

    def send_own(c):
        shift_copy(c).wait_recv()
        own_copy(c, 0).start()
        own_copy(c, 1).start()

    def forward(c):
        own_copy(c, 0).wait_recv()
        forward_copy(c, 0).start()
        own_copy(c, 1).wait_recv()
        forward_copy(c, 1).start()

    def build_picks():
        for copy in code_copies:
            copy.wait_recv()
        for half, towards in ((0, along_z), (1, along_x)):
            for source in range(4):
                index = 0 if source == 0 else half * 3 + source
                for step in range(4):
                    code = codes[index, pl.ds(towards(step), 1), :]
                    picks[half, source, step * 64 : step * 64 + 64, :] = jnp.where(
                        code == slot_iota, 1.0, 0.0
                    ).astype(BF16)

    def pick_and_send(c):
        half = lax.rem(c, 2)
        forward_copy(c, 0).wait_recv()
        forward_copy(c, 1).wait_recv()
        mine = x * (1 - half) + z * half
        for source, delta in ((0, 0), (1, 3), (2, 1), (3, 2)):
            block = shifted[c] if source == 0 else line[c, source - 1]
            place = lax.rem(mine + delta, 4)
            picked = jnp.dot(picks[half, source], block, preferred_element_type=F32).astype(BF16)
            for step in range(1, 4):
                outgoing[c, step - 1, place] = picked[step * 64 : step * 64 + 64]
            rows[c, z * (1 - half) + place * half, place * (1 - half) + x * half] = picked[:64]
        for h in range(2):

            @pl.when(half == h)
            def _():
                for step in range(1, 4):
                    out_copy(c, step, h).start()

    def activate():
        pre_load.wait()

        @pl.loop(1, 16)
        def _(step):
            tile_copy(step).wait_recv()

        mine = prob_tiles[:, pl.ds(me // 2, 1), :].reshape(16, 128)
        mine = jnp.where(lax.rem(me, 2) == 1, pltpu.roll(mine, 64, 1), mine)
        turned = jnp.concatenate([mine] * 8, axis=0).T
        for j in range(16):
            row_prob[j * 64 : j * 64 + 64, :] = jnp.broadcast_to(
                turned[:64, j : j + 1], (64, 128)
            )

        @pl.loop(0, 8)
        def _(b):
            here = pl.ds(pl.multiple_of(b * 128, 128), 128)
            factor = row_prob[here, :]
            for q in range(8):
                gate = pre[here, q * 128 : q * 128 + 128].astype(F32)
                up = pre[here, 1024 + q * 128 : 1024 + q * 128 + 128].astype(F32)
                value = gate * jax.nn.sigmoid(gate) * up
                hidden[here, q * 128 : q * 128 + 128] = value.astype(BF16)
                scaled_t[q * 128 : q * 128 + 128, here] = (value * factor).T.astype(BF16)

        hidden_grad[...] = jnp.zeros_like(hidden_grad)

    def arrived(c):
        for step in range(1, 4):
            out_copy(c, step, 0).wait_recv()

    def add_input_terms(c):
        weight_load(c).wait()

        @pl.loop(0, 4)
        def _(b):
            here = pl.ds(pl.multiple_of(b * 256, 256), 256)
            hidden_grad[here, :] += lax.dot_general(
                rows[c, b].reshape(256, COLS),
                weight[c],
                (((1,), (1,)), ((), ())),
                preferred_element_type=F32,
            )

    def weight_terms(c):
        there = pl.ds(pl.multiple_of(c * COLS, COLS), COLS)
        block = rows[c].reshape(1024, COLS)

        @pl.loop(0, 4)
        def _(b):
            here = pl.ds(pl.multiple_of(b * 256, 256), 256)
            down_grad[here, there] = jnp.dot(
                scaled_t[here, :], block, preferred_element_type=F32
            ).astype(BF16)

    @pl.loop(0, chunks + LAG)
    def _(i):
        @pl.when(i < chunks)
        def _():
            send_own(i)

        @pl.when((i >= 1) & (i < chunks + 1))
        def _():
            forward(i - 1)

        @pl.when(i == 1)
        def _():
            build_picks()

        @pl.when((i >= 2) & (i < chunks + 2))
        def _():
            pick_and_send(i - 2)

        @pl.when(i == 2)
        def _():
            activate()

        @pl.when(i >= LAG)
        def _():
            arrived(i - LAG)
            add_input_terms(i - LAG)

            @pl.when(i < chunks + LAG - 1)
            def _():
                weight_terms(i - LAG)

    @pl.loop(0, 8)
    def _(b):
        here = pl.ds(pl.multiple_of(b * 128, 128), 128)
        factor = row_prob[here, :]
        total = jnp.zeros((128, 128), F32)
        for q in range(8):
            value = hidden_grad[here, q * 128 : q * 128 + 128]
            total = total + hidden[here, q * 128 : q * 128 + 128].astype(F32) * value
            hidden_grad[here, q * 128 : q * 128 + 128] = value * factor
        back_tile[pl.ds(b, 1), :] = jnp.sum(total.T, axis=0, keepdims=True)

    def back_copy(step):
        return remote(
            back_tile,
            back_tiles.at[me],
            back_send.at[step],
            back_recv.at[step],
            (pipe, lax.rem(me + step, 16)),
        )

    @pl.loop(1, 16)
    def _(step):
        back_copy(step).start()

    back_tiles[me] = back_tile[...]
    weight_terms(chunks - 1)

    @pl.loop(1, 16)
    def _(step):
        back_copy(step).wait_recv()

    mine = back_tiles[:, pl.ds(me // 2, 1), :].reshape(16, 128)
    other = pltpu.roll(mine, 64, 1)
    low = lax.broadcasted_iota(jnp.int32, (16, 128), 1) < 64
    odd = lax.rem(me, 2) == 1
    both = jnp.where(low == jnp.logical_not(odd), mine, other)
    spread = jnp.where(diagonal, jnp.concatenate([both] * 8, axis=1), 0.0)
    high = spread.astype(BF16)
    rest = spread - high.astype(F32)
    middle = rest.astype(BF16)
    small = (rest - middle.astype(F32)).astype(BF16)
    pieces = jnp.dot(
        jnp.concatenate([high, middle, small], axis=0), own_picks[...], preferred_element_type=F32
    )
    token_grad = pieces[:16] + pieces[16:32] + pieces[32:]
    result = jnp.zeros((8, 256), F32)
    for e in range(16):
        result = result + jnp.where(route_ref[...] == e, token_grad[e : e + 1, :], 0.0)
    prob_grad[...] = result

    for copy in code_copies:
        copy.wait_send()

    @pl.loop(1, 16)
    def _(step):
        tile_copy(step).wait_send()
        back_copy(step).wait_send()

    @pl.loop(0, chunks)
    def _(c):
        shift_copy(c).wait_send()
        for side in range(2):
            own_copy(c, side).wait_send()
            forward_copy(c, side).wait_send()
        for step in range(1, 4):
            out_copy(c, step, 0).wait_send()


def exchange(grad, route_t, prob_t, pre, weight):
    chunks = grad.shape[1] // COLS
    hbm = pl.BlockSpec(memory_space=pl.ANY)
    vmem = pl.BlockSpec(memory_space=pltpu.VMEM)
    dma = pltpu.SemaphoreType.DMA
    return pl.pallas_call(
        exchange_kernel,
        out_shape=(
            jax.ShapeDtypeStruct((1024, 1024), F32),
            jax.ShapeDtypeStruct((1024, chunks * COLS), BF16),
            jax.ShapeDtypeStruct((8, 256), F32),
        ),
        in_specs=[hbm, vmem, vmem, hbm, hbm],
        out_specs=(vmem, vmem, vmem),
        scratch_shapes=[
            pltpu.VMEM((chunks, 256, COLS), BF16),
            pltpu.VMEM((chunks, 3, 256, COLS), BF16),
            pltpu.VMEM((chunks, 3, 4, 64, COLS), BF16),
            pltpu.VMEM((chunks, 4, 4, 64, COLS), BF16),
            pltpu.VMEM((chunks, 1024, COLS), BF16),
            pltpu.VMEM((1024, 2048), BF16),
            pltpu.VMEM((1024, 1024), BF16),
            pltpu.VMEM((1024, 1024), BF16),
            pltpu.VMEM((7, 16, 256), F32),
            pltpu.VMEM((2, 4, 256, 256), BF16),
            pltpu.VMEM((1024, 256), BF16),
            pltpu.VMEM((16, 8, 128), F32),
            pltpu.VMEM((8, 128), F32),
            pltpu.VMEM((16, 8, 128), F32),
            pltpu.VMEM((1024, 128), F32),
            dma((chunks + 1,)),
            dma((chunks,)),
            dma((chunks,)),
            dma((chunks, 2)),
            dma((chunks, 2)),
            dma((chunks, 4)),
            dma((chunks, 3)),
            dma((chunks, 3)),
            dma((6,)),
            dma((6,)),
            dma((16,)),
            dma((16,)),
            dma((16,)),
            dma((16,)),
        ],
        compiler_params=pltpu.CompilerParams(
            collective_id=0, has_side_effects=True, vmem_limit_bytes=62 * 2**20
        ),
        name="exchange",
    )(grad, route_t, prob_t, pre, weight)


def input_grad_kernel(hidden_grad, pre, out):
    half = pre.shape[1] // 2
    gate = pre[:, :half].astype(F32)
    up = pre[:, half:].astype(F32)
    sig = jax.nn.sigmoid(gate)
    grad = hidden_grad[...]
    out[:, :half] = (grad * up * sig * (1.0 + gate * (1.0 - sig))).astype(BF16)
    out[:, half:] = (grad * (gate * sig)).astype(BF16)


def input_grad(hidden_grad, pre):
    block = 128
    return pl.pallas_call(
        input_grad_kernel,
        out_shape=jax.ShapeDtypeStruct(pre.shape, BF16),
        grid=(pre.shape[0] // block,),
        in_specs=[
            pl.BlockSpec((block, pre.shape[1] // 2), lambda i: (i, 0)),
            pl.BlockSpec((block, pre.shape[1]), lambda i: (i, 0)),
        ],
        out_specs=pl.BlockSpec((block, pre.shape[1]), lambda i: (i, 0)),
        name="input_grad",
    )(hidden_grad, pre)


def on_device(boundary_grad, route_ids, route_probs, saved_preact, down_weight):
    pre = saved_preact[0, 0]
    hidden_grad, down_grad, prob_grad = exchange(
        boundary_grad[0], route_ids[0].T, route_probs[0].T, pre, down_weight[0, 0]
    )
    return (input_grad(hidden_grad, pre)[None, None], down_grad[None, None], prob_grad.T[None])


def solution(mesh):
    placed = (
        P("pipe", "expert", None),
        P("pipe", "expert", None),
        P("pipe", "expert", None),
        P("pipe", "expert", None, None),
        P("pipe", "expert", None, None),
    )
    return jax.shard_map(
        on_device,
        mesh=mesh,
        in_specs=placed,
        out_specs=(
            P("pipe", "expert", None, None),
            P("pipe", "expert", None, None),
            P("pipe", "expert", None),
        ),
        check_vma=False,
    )
```

```python
import functools

import jax
import jax.numpy as jnp
from jax import lax
from jax.experimental import pallas as pl
from jax.experimental.pallas import tpu as pltpu
from jax.sharding import PartitionSpec as P

MESH = pl.DeviceIdType.MESH
F32 = jnp.float32
BF16 = jnp.bfloat16
COLS = 256
SHIFTS = 4
FORWARD_LAG = 3
PICK_LAG = 6
LAG = 10


def exchange_kernel(
    grad_hbm,
    route_ref,
    prob_ref,
    pre_hbm,
    weight_hbm,
    pre,
    down_grad,
    prob_grad,
    hidden_grad,
    shifted,
    line,
    outgoing,
    rows,
    weight,
    hidden,
    scaled_t,
    codes,
    picks,
    own_picks,
    prob_tiles,
    back_tile,
    back_tiles,
    row_prob,
    load_sem,
    shift_send,
    shift_recv,
    own_send,
    forward_send,
    line_recv,
    out_send,
    rows_recv,
    code_send,
    code_recv,
    tile_send,
    tile_recv,
    back_send,
    back_recv,
):
    chunks = shifted.shape[0]
    pipe = lax.axis_index("pipe")
    me = lax.axis_index("expert")
    z, x = me // 4, me % 4
    before = lax.rem(pipe + 7, 8)

    def along_x(step):
        return z * 4 + lax.rem(x + step, 4)

    def along_z(step):
        return lax.rem(z + step, 4) * 4 + x

    def first_axis(half, step):
        return along_x(step) * (1 - half) + along_z(step) * half

    def second_axis(half, step):
        return along_z(step) * (1 - half) + along_x(step) * half

    def remote(src, dst, send, recv, device):
        return pltpu.make_async_remote_copy(
            src_ref=src,
            dst_ref=dst,
            send_sem=send,
            recv_sem=recv,
            device_id=device,
            device_id_type=MESH,
        )

    barrier = pltpu.get_barrier_semaphore()
    for step in range(1, 16):
        pl.semaphore_signal(
            barrier, inc=1, device_id=(pipe, lax.rem(me + step, 16)), device_id_type=MESH
        )
    for step in (1, 7):
        pl.semaphore_signal(
            barrier, inc=1, device_id=(lax.rem(pipe + step, 8), me), device_id_type=MESH
        )

    pre_load = pltpu.make_async_copy(pre_hbm, pre, load_sem.at[chunks])
    pre_load.start()

    def weight_load(c):
        return pltpu.make_async_copy(
            weight_hbm.at[:, pl.ds(pl.multiple_of(c * COLS, COLS), COLS)],
            weight.at[c],
            load_sem.at[c],
        )

    @pl.loop(0, chunks)
    def _(c):
        weight_load(c).start()

    expert_iota = lax.broadcasted_iota(jnp.int32, (16, 256), 0)
    member = jnp.zeros((16, 256), F32)
    token_prob = jnp.zeros((16, 256), F32)
    for k in range(8):
        hit = route_ref[k : k + 1, :] == expert_iota
        member = member + jnp.where(hit, 1.0, 0.0)
        token_prob = token_prob + jnp.where(hit, prob_ref[k : k + 1, :].astype(F32), 0.0)
    earlier = (
        lax.broadcasted_iota(jnp.int32, (256, 256), 0)
        <= lax.broadcasted_iota(jnp.int32, (256, 256), 1)
    )
    rank = jnp.dot(
        member.astype(BF16), jnp.where(earlier, 1.0, 0.0).astype(BF16), preferred_element_type=F32
    )
    codes[0] = jnp.where(member > 0.5, rank - 1.0, -1.0)
    slot_iota = lax.broadcasted_iota(jnp.int32, (64, 256), 0).astype(F32)
    for e in range(16):
        own_picks[e * 64 : e * 64 + 64, :] = jnp.where(
            codes[0, e : e + 1, :] == slot_iota, 1.0, 0.0
        ).astype(BF16)
    diagonal = (
        lax.broadcasted_iota(jnp.int32, (16, 1024), 1) // 64
        == lax.broadcasted_iota(jnp.int32, (16, 1024), 0)
    )
    slot_probs = lax.dot_general(
        token_prob.astype(BF16),
        own_picks[...],
        (((1,), (1,)), ((), ())),
        preferred_element_type=F32,
    )
    slot_probs = jnp.sum(jnp.where(diagonal, slot_probs, 0.0), axis=0, keepdims=True)
    for r in range(8):
        prob_tiles[me, r : r + 1, :] = slot_probs[:, r * 128 : r * 128 + 128]

    pl.semaphore_wait(barrier, 17)

    def shift_copy(c):
        return remote(
            grad_hbm.at[:, pl.ds(pl.multiple_of(c * COLS, COLS), COLS)],
            shifted.at[c],
            shift_send.at[c],
            shift_recv.at[c],
            (before, me),
        )

    @pl.loop(0, SHIFTS)
    def _(c):
        shift_copy(c).start()

    code_copies = []
    for half, towards in ((0, along_x), (1, along_z)):
        for slot, step in ((1, 1), (2, 3), (3, 2)):
            index = half * 3 + slot
            code_copies.append(
                remote(
                    codes.at[0],
                    codes.at[index],
                    code_send.at[index - 1],
                    code_recv.at[index - 1],
                    (pipe, towards(step)),
                )
            )
    for copy in code_copies:
        copy.start()

    def tile_copy(step):
        return remote(
            prob_tiles.at[me],
            prob_tiles.at[me],
            tile_send.at[step],
            tile_recv.at[step],
            (pipe, lax.rem(me + step, 16)),
        )

    @pl.loop(1, 16)
    def _(step):
        tile_copy(step).start()

    def own_copy(c, side):
        half = lax.rem(c, 2)
        return remote(
            shifted.at[c],
            line.at[c, side],
            own_send.at[c, side],
            line_recv.at[c, side],
            (pipe, first_axis(half, 1 if side == 0 else 3)),
        )

    def forward_copy(c, side):
        half = lax.rem(c, 2)
        part = pl.ds(side * 128, 128)
        return remote(
            line.at[c, side, part],
            line.at[c, 2, part],
            forward_send.at[c, side],
            line_recv.at[c, 2 + side],
            (pipe, first_axis(half, 1 if side == 0 else 3)),
        )

    def out_copy(c, step, half):
        target = rows.at[c, z] if half == 0 else rows.at[c, :, x]
        return remote(
            outgoing.at[c, step - 1],
            target,
            out_send.at[c, step - 1],
            rows_recv.at[c, step - 1],
            (pipe, second_axis(half, step)),
        )

    def send_own(c):
        shift_copy(c).wait_recv()

        @pl.when(c + SHIFTS < chunks)
        def _():
            shift_copy(c + SHIFTS).start()

        own_copy(c, 0).start()
        own_copy(c, 1).start()

    def forward(c):
        own_copy(c, 0).wait_recv()
        forward_copy(c, 0).start()
        own_copy(c, 1).wait_recv()
        forward_copy(c, 1).start()

    def build_picks():
        for copy in code_copies:
            copy.wait_recv()
        for half, towards in ((0, along_z), (1, along_x)):
            for source in range(4):
                index = 0 if source == 0 else half * 3 + source
                for step in range(4):
                    code = codes[index, pl.ds(towards(step), 1), :]
                    picks[half, source, step * 64 : step * 64 + 64, :] = jnp.where(
                        code == slot_iota, 1.0, 0.0
                    ).astype(BF16)

    def pick_and_send(c):
        half = lax.rem(c, 2)
        forward_copy(c, 0).wait_recv()
        forward_copy(c, 1).wait_recv()
        mine = x * (1 - half) + z * half
        for source, delta in ((0, 0), (1, 3), (2, 1), (3, 2)):
            block = shifted[c] if source == 0 else line[c, source - 1]
            place = lax.rem(mine + delta, 4)
            picked = jnp.dot(picks[half, source], block, preferred_element_type=F32).astype(BF16)
            for step in range(1, 4):
                outgoing[c, step - 1, place] = picked[step * 64 : step * 64 + 64]
            rows[c, z * (1 - half) + place * half, place * (1 - half) + x * half] = picked[:64]
        for h in range(2):

            @pl.when(half == h)
            def _():
                for step in range(1, 4):
                    out_copy(c, step, h).start()

    def activate():
        pre_load.wait()

        @pl.loop(1, 16)
        def _(step):
            tile_copy(step).wait_recv()

        mine = prob_tiles[:, pl.ds(me // 2, 1), :].reshape(16, 128)
        mine = jnp.where(lax.rem(me, 2) == 1, pltpu.roll(mine, 64, 1), mine)
        turned = jnp.concatenate([mine] * 8, axis=0).T
        for j in range(16):
            row_prob[j * 64 : j * 64 + 64, :] = jnp.broadcast_to(
                turned[:64, j : j + 1], (64, 128)
            )

        @pl.loop(0, 8)
        def _(b):
            here = pl.ds(pl.multiple_of(b * 128, 128), 128)
            factor = row_prob[here, :]
            for q in range(8):
                gate = pre[here, q * 128 : q * 128 + 128].astype(F32)
                up = pre[here, 1024 + q * 128 : 1024 + q * 128 + 128].astype(F32)
                sig = jax.nn.sigmoid(gate)
                silu = gate * sig
                value = silu * up
                pre[here, q * 128 : q * 128 + 128] = (
                    up * sig * (1.0 + gate * (1.0 - sig))
                ).astype(BF16)
                pre[here, 1024 + q * 128 : 1024 + q * 128 + 128] = silu.astype(BF16)
                hidden[here, q * 128 : q * 128 + 128] = value.astype(BF16)
                scaled_t[q * 128 : q * 128 + 128, here] = (value * factor).T.astype(BF16)

        hidden_grad[...] = jnp.zeros_like(hidden_grad)

    def arrived(c):
        for step in range(1, 4):
            out_copy(c, step, 0).wait_recv()

    def add_input_terms(c):
        weight_load(c).wait()

        @pl.loop(0, 4)
        def _(b):
            here = pl.ds(pl.multiple_of(b * 256, 256), 256)
            hidden_grad[here, :] += lax.dot_general(
                rows[c, b].reshape(256, COLS),
                weight[c],
                (((1,), (1,)), ((), ())),
                preferred_element_type=F32,
            )

    def weight_terms(c):
        there = pl.ds(pl.multiple_of(c * COLS, COLS), COLS)
        block = rows[c].reshape(1024, COLS)

        @pl.loop(0, 4)
        def _(b):
            here = pl.ds(pl.multiple_of(b * 256, 256), 256)
            down_grad[here, there] = jnp.dot(
                scaled_t[here, :], block, preferred_element_type=F32
            ).astype(BF16)

    @pl.loop(0, chunks + LAG)
    def _(i):
        @pl.when(i < chunks)
        def _():
            send_own(i)

        @pl.when((i >= FORWARD_LAG) & (i < chunks + FORWARD_LAG))
        def _():
            forward(i - FORWARD_LAG)

        @pl.when(i == PICK_LAG - 1)
        def _():
            build_picks()
            activate()

        @pl.when((i >= PICK_LAG) & (i < chunks + PICK_LAG))
        def _():
            pick_and_send(i - PICK_LAG)

        @pl.when(i >= LAG)
        def _():
            arrived(i - LAG)
            add_input_terms(i - LAG)

            @pl.when(i < chunks + LAG - 1)
            def _():
                weight_terms(i - LAG)

    @pl.loop(0, 8)
    def _(b):
        here = pl.ds(pl.multiple_of(b * 128, 128), 128)
        factor = row_prob[here, :]
        total = jnp.zeros((128, 128), F32)
        for q in range(8):
            value = hidden_grad[here, q * 128 : q * 128 + 128]
            total = total + hidden[here, q * 128 : q * 128 + 128].astype(F32) * value
        back_tile[pl.ds(b, 1), :] = jnp.sum(total.T, axis=0, keepdims=True)

    def back_copy(step):
        return remote(
            back_tile,
            back_tiles.at[me],
            back_send.at[step],
            back_recv.at[step],
            (pipe, lax.rem(me + step, 16)),
        )

    @pl.loop(1, 16)
    def _(step):
        back_copy(step).start()

    back_tiles[me] = back_tile[...]
    weight_terms(chunks - 1)

    @pl.loop(0, 8)
    def _(b):
        here = pl.ds(pl.multiple_of(b * 128, 128), 128)
        factor = row_prob[here, :]
        for q in range(8):
            value = hidden_grad[here, q * 128 : q * 128 + 128] * factor
            for first in (q * 128, 1024 + q * 128):
                pre[here, first : first + 128] = (
                    value * pre[here, first : first + 128].astype(F32)
                ).astype(BF16)

    @pl.loop(1, 16)
    def _(step):
        back_copy(step).wait_recv()

    mine = back_tiles[:, pl.ds(me // 2, 1), :].reshape(16, 128)
    other = pltpu.roll(mine, 64, 1)
    low = lax.broadcasted_iota(jnp.int32, (16, 128), 1) < 64
    odd = lax.rem(me, 2) == 1
    both = jnp.where(low == jnp.logical_not(odd), mine, other)
    spread = jnp.where(diagonal, jnp.concatenate([both] * 8, axis=1), 0.0)
    high = spread.astype(BF16)
    rest = spread - high.astype(F32)
    middle = rest.astype(BF16)
    small = (rest - middle.astype(F32)).astype(BF16)
    pieces = jnp.dot(
        jnp.concatenate([high, middle, small], axis=0), own_picks[...], preferred_element_type=F32
    )
    token_grad = pieces[:16] + pieces[16:32] + pieces[32:]
    result = jnp.zeros((8, 256), F32)
    for e in range(16):
        result = result + jnp.where(route_ref[...] == e, token_grad[e : e + 1, :], 0.0)
    prob_grad[...] = result

    for copy in code_copies:
        copy.wait_send()

    @pl.loop(1, 16)
    def _(step):
        tile_copy(step).wait_send()
        back_copy(step).wait_send()

    @pl.loop(0, chunks)
    def _(c):
        shift_copy(c).wait_send()
        for side in range(2):
            own_copy(c, side).wait_send()
            forward_copy(c, side).wait_send()
        for step in range(1, 4):
            out_copy(c, step, 0).wait_send()


def exchange(grad, route_t, prob_t, pre, weight):
    chunks = grad.shape[1] // COLS
    hbm = pl.BlockSpec(memory_space=pl.ANY)
    vmem = pl.BlockSpec(memory_space=pltpu.VMEM)
    dma = pltpu.SemaphoreType.DMA
    return pl.pallas_call(
        exchange_kernel,
        out_shape=(
            pltpu.VMEM((1024, 2048), BF16),
            pltpu.VMEM((1024, chunks * COLS), BF16),
            pltpu.VMEM((8, 256), F32),
        ),
        in_specs=[hbm, vmem, vmem, hbm, hbm],
        out_specs=(vmem, vmem, vmem),
        scratch_shapes=[
            pltpu.VMEM((1024, 1024), F32),
            pltpu.VMEM((chunks, 256, COLS), BF16),
            pltpu.VMEM((chunks, 3, 256, COLS), BF16),
            pltpu.VMEM((chunks, 3, 4, 64, COLS), BF16),
            pltpu.VMEM((chunks, 4, 4, 64, COLS), BF16),
            pltpu.VMEM((chunks, 1024, COLS), BF16),
            pltpu.VMEM((1024, 1024), BF16),
            pltpu.VMEM((1024, 1024), BF16),
            pltpu.VMEM((7, 16, 256), F32),
            pltpu.VMEM((2, 4, 256, 256), BF16),
            pltpu.VMEM((1024, 256), BF16),
            pltpu.VMEM((16, 8, 128), F32),
            pltpu.VMEM((8, 128), F32),
            pltpu.VMEM((16, 8, 128), F32),
            pltpu.VMEM((1024, 128), F32),
            dma((chunks + 1,)),
            dma((chunks,)),
            dma((chunks,)),
            dma((chunks, 2)),
            dma((chunks, 2)),
            dma((chunks, 4)),
            dma((chunks, 3)),
            dma((chunks, 3)),
            dma((6,)),
            dma((6,)),
            dma((16,)),
            dma((16,)),
            dma((16,)),
            dma((16,)),
        ],
        compiler_params=pltpu.CompilerParams(
            collective_id=0, has_side_effects=True, vmem_limit_bytes=50 * 2**20
        ),
        name="exchange",
    )(grad, route_t, prob_t, pre, weight)


def store_kernel(*refs):
    count = len(refs) // 2
    copies = [
        pltpu.make_async_copy(refs[i], refs[count + i], refs[-1].at[i]) for i in range(count)
    ]
    for copy in copies:
        copy.start()
    for copy in copies:
        copy.wait()


def store(*results):
    return pl.pallas_call(
        store_kernel,
        out_shape=tuple(jax.ShapeDtypeStruct(r.shape, r.dtype) for r in results),
        in_specs=[pl.BlockSpec(memory_space=pltpu.VMEM)] * len(results),
        out_specs=tuple(pl.BlockSpec(memory_space=pl.ANY) for _ in results),
        scratch_shapes=[pltpu.SemaphoreType.DMA((len(results),))],
        compiler_params=pltpu.CompilerParams(vmem_limit_bytes=2**20),
        name="store",
    )(*(pltpu.with_memory_space_constraint(r, pltpu.VMEM) for r in results))


def on_device(boundary_grad, route_ids, route_probs, saved_preact, down_weight):
    preact_grad, down_grad, prob_grad = store(
        *exchange(
            boundary_grad[0],
            route_ids[0].T,
            route_probs[0].T,
            saved_preact[0, 0],
            down_weight[0, 0],
        )
    )
    return (preact_grad[None, None], down_grad[None, None], prob_grad.T[None])


def solution(mesh):
    placed = (
        P("pipe", "expert", None),
        P("pipe", "expert", None),
        P("pipe", "expert", None),
        P("pipe", "expert", None, None),
        P("pipe", "expert", None, None),
    )
    return jax.shard_map(
        on_device,
        mesh=mesh,
        in_specs=placed,
        out_specs=(
            P("pipe", "expert", None, None),
            P("pipe", "expert", None, None),
            P("pipe", "expert", None),
        ),
        check_vma=False,
    )
```

```python
import functools

import jax
import jax.numpy as jnp
from jax import lax
from jax.experimental import pallas as pl
from jax.experimental.pallas import tpu as pltpu
from jax.sharding import PartitionSpec as P

MESH = pl.DeviceIdType.MESH
F32 = jnp.float32
BF16 = jnp.bfloat16
COLS = 256
SHIFTS = 4
FORWARD_LAG = 3
PICK_LAG = 6
LAG = 9


def exchange_kernel(
    grad_hbm,
    route_hbm,
    prob_hbm,
    pre_hbm,
    weight_hbm,
    pre,
    down_grad,
    prob_grad,
    route_ref,
    prob_ref,
    hidden_grad,
    shifted,
    line,
    outgoing,
    rows,
    weight,
    hidden,
    scaled_t,
    codes,
    picks,
    own_picks,
    prob_tiles,
    back_tile,
    back_tiles,
    row_prob,
    load_sem,
    shift_send,
    shift_recv,
    own_send,
    forward_send,
    line_recv,
    out_send,
    rows_recv,
    code_send,
    code_recv,
    tile_send,
    tile_recv,
    back_send,
    back_recv,
):
    chunks = shifted.shape[0]
    pipe = lax.axis_index("pipe")
    me = lax.axis_index("expert")
    z, x = me // 4, me % 4
    before = lax.rem(pipe + 7, 8)

    def along_x(step):
        return z * 4 + lax.rem(x + step, 4)

    def along_z(step):
        return lax.rem(z + step, 4) * 4 + x

    def first_axis(half, step):
        return along_x(step) * (1 - half) + along_z(step) * half

    def second_axis(half, step):
        return along_z(step) * (1 - half) + along_x(step) * half

    def remote(src, dst, send, recv, device):
        return pltpu.make_async_remote_copy(
            src_ref=src,
            dst_ref=dst,
            send_sem=send,
            recv_sem=recv,
            device_id=device,
            device_id_type=MESH,
        )

    barrier = pltpu.get_barrier_semaphore()
    for step in range(1, 16):
        pl.semaphore_signal(
            barrier, inc=1, device_id=(pipe, lax.rem(me + step, 16)), device_id_type=MESH
        )
    for step in (1, 7):
        pl.semaphore_signal(
            barrier, inc=1, device_id=(lax.rem(pipe + step, 8), me), device_id_type=MESH
        )

    small_loads = (
        pltpu.make_async_copy(route_hbm, route_ref, load_sem.at[chunks + 1]),
        pltpu.make_async_copy(prob_hbm, prob_ref, load_sem.at[chunks + 2]),
    )
    for load in small_loads:
        load.start()
    pre_load = pltpu.make_async_copy(pre_hbm, pre, load_sem.at[chunks])
    pre_load.start()

    def weight_load(c):
        return pltpu.make_async_copy(
            weight_hbm.at[:, pl.ds(pl.multiple_of(c * COLS, COLS), COLS)],
            weight.at[c],
            load_sem.at[c],
        )

    @pl.loop(0, chunks)
    def _(c):
        weight_load(c).start()

    pl.semaphore_wait(barrier, 17)

    def shift_copy(c):
        return remote(
            grad_hbm.at[:, pl.ds(pl.multiple_of(c * COLS, COLS), COLS)],
            shifted.at[c],
            shift_send.at[c],
            shift_recv.at[c],
            (before, me),
        )

    @pl.loop(0, SHIFTS)
    def _(c):
        shift_copy(c).start()

    for load in small_loads:
        load.wait()

    expert_iota = lax.broadcasted_iota(jnp.int32, (16, 256), 0)
    member = jnp.zeros((16, 256), F32)
    token_prob = jnp.zeros((16, 256), F32)
    for k in range(8):
        hit = route_ref[k : k + 1, :] == expert_iota
        member = member + jnp.where(hit, 1.0, 0.0)
        token_prob = token_prob + jnp.where(hit, prob_ref[k : k + 1, :].astype(F32), 0.0)
    earlier = (
        lax.broadcasted_iota(jnp.int32, (256, 256), 0)
        <= lax.broadcasted_iota(jnp.int32, (256, 256), 1)
    )
    rank = jnp.dot(
        member.astype(BF16), jnp.where(earlier, 1.0, 0.0).astype(BF16), preferred_element_type=F32
    )
    codes[0] = jnp.where(member > 0.5, rank - 1.0, -1.0)
    slot_iota = lax.broadcasted_iota(jnp.int32, (64, 256), 0).astype(F32)
    for e in range(16):
        own_picks[e * 64 : e * 64 + 64, :] = jnp.where(
            codes[0, e : e + 1, :] == slot_iota, 1.0, 0.0
        ).astype(BF16)
    diagonal = (
        lax.broadcasted_iota(jnp.int32, (16, 1024), 1) // 64
        == lax.broadcasted_iota(jnp.int32, (16, 1024), 0)
    )
    slot_probs = lax.dot_general(
        token_prob.astype(BF16),
        own_picks[...],
        (((1,), (1,)), ((), ())),
        preferred_element_type=F32,
    )
    slot_probs = jnp.sum(jnp.where(diagonal, slot_probs, 0.0), axis=0, keepdims=True)
    for r in range(8):
        prob_tiles[me, r : r + 1, :] = slot_probs[:, r * 128 : r * 128 + 128]

    code_copies = []
    for half, towards in ((0, along_x), (1, along_z)):
        for slot, step in ((1, 1), (2, 3), (3, 2)):
            index = half * 3 + slot
            code_copies.append(
                remote(
                    codes.at[0],
                    codes.at[index],
                    code_send.at[index - 1],
                    code_recv.at[index - 1],
                    (pipe, towards(step)),
                )
            )
    for copy in code_copies:
        copy.start()

    def tile_copy(step):
        return remote(
            prob_tiles.at[me],
            prob_tiles.at[me],
            tile_send.at[step],
            tile_recv.at[step],
            (pipe, lax.rem(me + step, 16)),
        )

    @pl.loop(1, 16)
    def _(step):
        tile_copy(step).start()

    def own_copy(c, side):
        half = lax.rem(c, 2)
        return remote(
            shifted.at[c],
            line.at[c, side],
            own_send.at[c, side],
            line_recv.at[c, side],
            (pipe, first_axis(half, 1 if side == 0 else 3)),
        )

    def forward_copy(c, side):
        half = lax.rem(c, 2)
        part = pl.ds(side * 128, 128)
        return remote(
            line.at[c, side, part],
            line.at[c, 2, part],
            forward_send.at[c, side],
            line_recv.at[c, 2 + side],
            (pipe, first_axis(half, 1 if side == 0 else 3)),
        )

    def out_copy(c, step, half):
        target = rows.at[c, z] if half == 0 else rows.at[c, :, x]
        return remote(
            outgoing.at[c, step - 1],
            target,
            out_send.at[c, step - 1],
            rows_recv.at[c, step - 1],
            (pipe, second_axis(half, step)),
        )

    def send_own(c):
        shift_copy(c).wait_recv()

        @pl.when(c + SHIFTS < chunks)
        def _():
            shift_copy(c + SHIFTS).start()

        own_copy(c, 0).start()
        own_copy(c, 1).start()

    def forward(c):
        own_copy(c, 0).wait_recv()
        forward_copy(c, 0).start()
        own_copy(c, 1).wait_recv()
        forward_copy(c, 1).start()

    def build_picks():
        for copy in code_copies:
            copy.wait_recv()
        for half, towards in ((0, along_z), (1, along_x)):
            for source in range(4):
                index = 0 if source == 0 else half * 3 + source
                for step in range(4):
                    code = codes[index, pl.ds(towards(step), 1), :]
                    picks[half, source, step * 64 : step * 64 + 64, :] = jnp.where(
                        code == slot_iota, 1.0, 0.0
                    ).astype(BF16)

    def pick_and_send(c):
        half = lax.rem(c, 2)
        forward_copy(c, 0).wait_recv()
        forward_copy(c, 1).wait_recv()
        mine = x * (1 - half) + z * half
        for source, delta in ((0, 0), (1, 3), (2, 1), (3, 2)):
            block = shifted[c] if source == 0 else line[c, source - 1]
            place = lax.rem(mine + delta, 4)
            picked = jnp.dot(picks[half, source], block, preferred_element_type=F32).astype(BF16)
            for step in range(1, 4):
                outgoing[c, step - 1, place] = picked[step * 64 : step * 64 + 64]
            rows[c, z * (1 - half) + place * half, place * (1 - half) + x * half] = picked[:64]
        for h in range(2):

            @pl.when(half == h)
            def _():
                for step in range(1, 4):
                    out_copy(c, step, h).start()

    def spread_probs():
        pre_load.wait()

        @pl.loop(1, 16)
        def _(step):
            tile_copy(step).wait_recv()

        mine = prob_tiles[:, pl.ds(me // 2, 1), :].reshape(16, 128)
        mine = jnp.where(lax.rem(me, 2) == 1, pltpu.roll(mine, 64, 1), mine)
        turned = jnp.concatenate([mine] * 8, axis=0).T
        for j in range(16):
            row_prob[j * 64 : j * 64 + 64, :] = jnp.broadcast_to(
                turned[:64, j : j + 1], (64, 128)
            )

        hidden_grad[...] = jnp.zeros_like(hidden_grad)

    def activate(first):
        @pl.loop(first, first + 2)
        def _(b):
            here = pl.ds(pl.multiple_of(b * 128, 128), 128)
            factor = row_prob[here, :]
            for q in range(8):
                gate = pre[here, q * 128 : q * 128 + 128].astype(F32)
                up = pre[here, 1024 + q * 128 : 1024 + q * 128 + 128].astype(F32)
                sig = jax.nn.sigmoid(gate)
                silu = gate * sig
                value = silu * up
                pre[here, q * 128 : q * 128 + 128] = (
                    up * sig * (1.0 + gate * (1.0 - sig))
                ).astype(BF16)
                pre[here, 1024 + q * 128 : 1024 + q * 128 + 128] = silu.astype(BF16)
                hidden[here, q * 128 : q * 128 + 128] = value.astype(BF16)
                scaled_t[q * 128 : q * 128 + 128, here] = (value * factor).T.astype(BF16)

    def arrived(c):
        for step in range(1, 4):
            out_copy(c, step, 0).wait_recv()

    def add_input_terms(c):
        weight_load(c).wait()

        hidden_grad[...] += lax.dot_general(
            rows[c].reshape(1024, COLS),
            weight[c],
            (((1,), (1,)), ((), ())),
            preferred_element_type=F32,
        )

    def weight_terms(c):
        there = pl.ds(pl.multiple_of(c * COLS, COLS), COLS)
        down_grad[:, there] = jnp.dot(
            scaled_t[...], rows[c].reshape(1024, COLS), preferred_element_type=F32
        ).astype(BF16)

    @pl.loop(0, chunks + LAG)
    def _(i):
        @pl.when(i < chunks)
        def _():
            send_own(i)

        @pl.when((i >= FORWARD_LAG) & (i < chunks + FORWARD_LAG))
        def _():
            forward(i - FORWARD_LAG)

        @pl.when(i == PICK_LAG - 1)
        def _():
            build_picks()

        @pl.when(i == 3)
        def _():
            spread_probs()

        @pl.when((i >= 4) & (i < 8))
        def _():
            activate(2 * i - 8)

        @pl.when((i >= PICK_LAG) & (i < chunks + PICK_LAG))
        def _():
            pick_and_send(i - PICK_LAG)

        @pl.when(i >= LAG)
        def _():
            arrived(i - LAG)
            add_input_terms(i - LAG)

            @pl.when(i < chunks + LAG - 1)
            def _():
                weight_terms(i - LAG)

    @pl.loop(0, 8)
    def _(b):
        here = pl.ds(pl.multiple_of(b * 128, 128), 128)
        factor = row_prob[here, :]
        total = jnp.zeros((128, 128), F32)
        for q in range(8):
            value = hidden_grad[here, q * 128 : q * 128 + 128]
            total = total + hidden[here, q * 128 : q * 128 + 128].astype(F32) * value
        back_tile[pl.ds(b, 1), :] = jnp.sum(total.T, axis=0, keepdims=True)

    def back_copy(step):
        return remote(
            back_tile,
            back_tiles.at[me],
            back_send.at[step],
            back_recv.at[step],
            (pipe, lax.rem(me + step, 16)),
        )

    @pl.loop(1, 16)
    def _(step):
        back_copy(step).start()

    back_tiles[me] = back_tile[...]
    weight_terms(chunks - 1)

    @pl.loop(0, 8)
    def _(b):
        here = pl.ds(pl.multiple_of(b * 128, 128), 128)
        factor = row_prob[here, :]
        for q in range(8):
            value = hidden_grad[here, q * 128 : q * 128 + 128] * factor
            for first in (q * 128, 1024 + q * 128):
                pre[here, first : first + 128] = (
                    value * pre[here, first : first + 128].astype(F32)
                ).astype(BF16)

    @pl.loop(1, 16)
    def _(step):
        back_copy(step).wait_recv()

    mine = back_tiles[:, pl.ds(me // 2, 1), :].reshape(16, 128)
    other = pltpu.roll(mine, 64, 1)
    low = lax.broadcasted_iota(jnp.int32, (16, 128), 1) < 64
    odd = lax.rem(me, 2) == 1
    both = jnp.where(low == jnp.logical_not(odd), mine, other)
    spread = jnp.where(diagonal, jnp.concatenate([both] * 8, axis=1), 0.0)
    high = spread.astype(BF16)
    rest = spread - high.astype(F32)
    middle = rest.astype(BF16)
    small = (rest - middle.astype(F32)).astype(BF16)
    pieces = jnp.dot(
        jnp.concatenate([high, middle, small], axis=0), own_picks[...], preferred_element_type=F32
    )
    token_grad = pieces[:16] + pieces[16:32] + pieces[32:]
    result = jnp.zeros((8, 256), F32)
    for e in range(16):
        result = result + jnp.where(route_ref[...] == e, token_grad[e : e + 1, :], 0.0)
    prob_grad[...] = result

    for copy in code_copies:
        copy.wait_send()

    @pl.loop(1, 16)
    def _(step):
        tile_copy(step).wait_send()
        back_copy(step).wait_send()

    @pl.loop(0, chunks)
    def _(c):
        shift_copy(c).wait_send()
        for side in range(2):
            own_copy(c, side).wait_send()
            forward_copy(c, side).wait_send()
        for step in range(1, 4):
            out_copy(c, step, 0).wait_send()


def exchange(grad, route_t, prob_t, pre, weight):
    chunks = grad.shape[1] // COLS
    hbm = pl.BlockSpec(memory_space=pl.ANY)
    vmem = pl.BlockSpec(memory_space=pltpu.VMEM)
    dma = pltpu.SemaphoreType.DMA
    return pl.pallas_call(
        exchange_kernel,
        out_shape=(
            pltpu.VMEM((1024, 2048), BF16),
            pltpu.VMEM((1024, chunks * COLS), BF16),
            pltpu.VMEM((8, 256), F32),
        ),
        in_specs=[hbm] * 5,
        out_specs=(vmem, vmem, vmem),
        scratch_shapes=[
            pltpu.VMEM((8, 256), jnp.int32),
            pltpu.VMEM((8, 256), BF16),
            pltpu.VMEM((1024, 1024), F32),
            pltpu.VMEM((chunks, 256, COLS), BF16),
            pltpu.VMEM((chunks, 3, 256, COLS), BF16),
            pltpu.VMEM((chunks, 3, 4, 64, COLS), BF16),
            pltpu.VMEM((chunks, 4, 4, 64, COLS), BF16),
            pltpu.VMEM((chunks, 1024, COLS), BF16),
            pltpu.VMEM((1024, 1024), BF16),
            pltpu.VMEM((1024, 1024), BF16),
            pltpu.VMEM((7, 16, 256), F32),
            pltpu.VMEM((2, 4, 256, 256), BF16),
            pltpu.VMEM((1024, 256), BF16),
            pltpu.VMEM((16, 8, 128), F32),
            pltpu.VMEM((8, 128), F32),
            pltpu.VMEM((16, 8, 128), F32),
            pltpu.VMEM((1024, 128), F32),
            dma((chunks + 3,)),
            dma((chunks,)),
            dma((chunks,)),
            dma((chunks, 2)),
            dma((chunks, 2)),
            dma((chunks, 4)),
            dma((chunks, 3)),
            dma((chunks, 3)),
            dma((6,)),
            dma((6,)),
            dma((16,)),
            dma((16,)),
            dma((16,)),
            dma((16,)),
        ],
        compiler_params=pltpu.CompilerParams(
            collective_id=0, has_side_effects=True, vmem_limit_bytes=50 * 2**20
        ),
        name="exchange",
    )(grad, route_t, prob_t, pre, weight)


def store_kernel(*refs):
    count = len(refs) // 2
    copies = [
        pltpu.make_async_copy(refs[i], refs[count + i], refs[-1].at[i]) for i in range(count)
    ]
    for copy in copies:
        copy.start()
    for copy in copies:
        copy.wait()


def store(*results):
    return pl.pallas_call(
        store_kernel,
        out_shape=tuple(jax.ShapeDtypeStruct(r.shape, r.dtype) for r in results),
        in_specs=[pl.BlockSpec(memory_space=pltpu.VMEM)] * len(results),
        out_specs=tuple(pl.BlockSpec(memory_space=pl.ANY) for _ in results),
        scratch_shapes=[pltpu.SemaphoreType.DMA((len(results),))],
        compiler_params=pltpu.CompilerParams(vmem_limit_bytes=2**20),
        name="store",
    )(*(pltpu.with_memory_space_constraint(r, pltpu.VMEM) for r in results))


def on_device(boundary_grad, route_ids, route_probs, saved_preact, down_weight):
    preact_grad, down_grad, prob_grad = store(
        *exchange(
            boundary_grad[0],
            route_ids[0].T,
            route_probs[0].T,
            saved_preact[0, 0],
            down_weight[0, 0],
        )
    )
    return (preact_grad[None, None], down_grad[None, None], prob_grad.T[None])


def solution(mesh):
    placed = (
        P("pipe", "expert", None),
        P("pipe", "expert", None),
        P("pipe", "expert", None),
        P("pipe", "expert", None, None),
        P("pipe", "expert", None, None),
    )
    return jax.shard_map(
        on_device,
        mesh=mesh,
        in_specs=placed,
        out_specs=(
            P("pipe", "expert", None, None),
            P("pipe", "expert", None, None),
            P("pipe", "expert", None),
        ),
        check_vma=False,
    )
```

```python
import functools

import jax
import jax.numpy as jnp
from jax import lax
from jax.experimental import pallas as pl
from jax.experimental.pallas import tpu as pltpu
from jax.sharding import PartitionSpec as P

MESH = pl.DeviceIdType.MESH
F32 = jnp.float32
BF16 = jnp.bfloat16
COLS = 256
SHIFTS = 4
FORWARD_LAG = 3
PICK_LAG = 6
LAG = 9
DEFERRED = 2


def exchange_kernel(
    grad_hbm,
    route_hbm,
    prob_hbm,
    pre_hbm,
    weight_hbm,
    pre,
    down_grad,
    back,
    own_picks,
    route_ref,
    prob_ref,
    hidden_grad,
    shifted,
    line,
    outgoing,
    rows,
    weight,
    hidden,
    scaled_t,
    codes,
    picks,
    prob_tiles,
    back_tile,
    back_tiles,
    row_prob,
    load_sem,
    shift_send,
    shift_recv,
    own_send,
    forward_send,
    line_recv,
    out_send,
    rows_recv,
    code_send,
    code_recv,
    tile_send,
    tile_recv,
    back_send,
    back_recv,
):
    chunks = shifted.shape[0]
    pipe = lax.axis_index("pipe")
    me = lax.axis_index("expert")
    z, x = me // 4, me % 4
    before = lax.rem(pipe + 7, 8)

    def along_x(step):
        return z * 4 + lax.rem(x + step, 4)

    def along_z(step):
        return lax.rem(z + step, 4) * 4 + x

    def first_axis(half, step):
        return along_x(step) * (1 - half) + along_z(step) * half

    def second_axis(half, step):
        return along_z(step) * (1 - half) + along_x(step) * half

    def remote(src, dst, send, recv, device):
        return pltpu.make_async_remote_copy(
            src_ref=src,
            dst_ref=dst,
            send_sem=send,
            recv_sem=recv,
            device_id=device,
            device_id_type=MESH,
        )

    barrier = pltpu.get_barrier_semaphore()
    for step in range(1, 16):
        pl.semaphore_signal(
            barrier, inc=1, device_id=(pipe, lax.rem(me + step, 16)), device_id_type=MESH
        )
    for step in (1, 7):
        pl.semaphore_signal(
            barrier, inc=1, device_id=(lax.rem(pipe + step, 8), me), device_id_type=MESH
        )

    small_loads = (
        pltpu.make_async_copy(route_hbm, route_ref, load_sem.at[chunks + 1]),
        pltpu.make_async_copy(prob_hbm, prob_ref, load_sem.at[chunks + 2]),
    )
    for load in small_loads:
        load.start()
    pre_load = pltpu.make_async_copy(pre_hbm, pre, load_sem.at[chunks])
    pre_load.start()

    def weight_load(c):
        return pltpu.make_async_copy(
            weight_hbm.at[:, pl.ds(pl.multiple_of(c * COLS, COLS), COLS)],
            weight.at[c],
            load_sem.at[c],
        )

    @pl.loop(0, chunks)
    def _(c):
        weight_load(c).start()

    pl.semaphore_wait(barrier, 17)

    def shift_copy(c):
        return remote(
            grad_hbm.at[:, pl.ds(pl.multiple_of(c * COLS, COLS), COLS)],
            shifted.at[c],
            shift_send.at[c],
            shift_recv.at[c],
            (before, me),
        )

    @pl.loop(0, SHIFTS)
    def _(c):
        shift_copy(c).start()

    for load in small_loads:
        load.wait()

    expert_iota = lax.broadcasted_iota(jnp.int32, (16, 256), 0)
    member = jnp.zeros((16, 256), F32)
    token_prob = jnp.zeros((16, 256), F32)
    for k in range(8):
        hit = route_ref[k : k + 1, :] == expert_iota
        member = member + jnp.where(hit, 1.0, 0.0)
        token_prob = token_prob + jnp.where(hit, prob_ref[k : k + 1, :].astype(F32), 0.0)
    earlier = (
        lax.broadcasted_iota(jnp.int32, (256, 256), 0)
        <= lax.broadcasted_iota(jnp.int32, (256, 256), 1)
    )
    rank = jnp.dot(
        member.astype(BF16), jnp.where(earlier, 1.0, 0.0).astype(BF16), preferred_element_type=F32
    )
    codes[0] = jnp.where(member > 0.5, rank - 1.0, -1.0)
    slot_iota = lax.broadcasted_iota(jnp.int32, (64, 256), 0).astype(F32)
    for e in range(16):
        own_picks[e * 64 : e * 64 + 64, :] = jnp.where(
            codes[0, e : e + 1, :] == slot_iota, 1.0, 0.0
        ).astype(BF16)
    diagonal = (
        lax.broadcasted_iota(jnp.int32, (16, 1024), 1) // 64
        == lax.broadcasted_iota(jnp.int32, (16, 1024), 0)
    )
    slot_probs = lax.dot_general(
        token_prob.astype(BF16),
        own_picks[...],
        (((1,), (1,)), ((), ())),
        preferred_element_type=F32,
    )
    slot_probs = jnp.sum(jnp.where(diagonal, slot_probs, 0.0), axis=0, keepdims=True)
    for r in range(8):
        prob_tiles[me, r : r + 1, :] = slot_probs[:, r * 128 : r * 128 + 128]

    code_copies = []
    for half, towards in ((0, along_x), (1, along_z)):
        for slot, step in ((1, 1), (2, 3), (3, 2)):
            index = half * 3 + slot
            code_copies.append(
                remote(
                    codes.at[0],
                    codes.at[index],
                    code_send.at[index - 1],
                    code_recv.at[index - 1],
                    (pipe, towards(step)),
                )
            )
    for copy in code_copies:
        copy.start()

    def tile_copy(step):
        return remote(
            prob_tiles.at[me],
            prob_tiles.at[me],
            tile_send.at[step],
            tile_recv.at[step],
            (pipe, lax.rem(me + step, 16)),
        )

    @pl.loop(1, 16)
    def _(step):
        tile_copy(step).start()

    def own_copy(c, side):
        half = lax.rem(c, 2)
        return remote(
            shifted.at[c],
            line.at[c, side],
            own_send.at[c, side],
            line_recv.at[c, side],
            (pipe, first_axis(half, 1 if side == 0 else 3)),
        )

    def forward_copy(c, side):
        half = lax.rem(c, 2)
        part = pl.ds(side * 128, 128)
        return remote(
            line.at[c, side, part],
            line.at[c, 2, part],
            forward_send.at[c, side],
            line_recv.at[c, 2 + side],
            (pipe, first_axis(half, 1 if side == 0 else 3)),
        )

    def out_copy(c, step, half):
        target = rows.at[c, z] if half == 0 else rows.at[c, :, x]
        return remote(
            outgoing.at[c, step - 1],
            target,
            out_send.at[c, step - 1],
            rows_recv.at[c, step - 1],
            (pipe, second_axis(half, step)),
        )

    def send_own(c):
        shift_copy(c).wait_recv()

        @pl.when(c + SHIFTS < chunks)
        def _():
            shift_copy(c + SHIFTS).start()

        own_copy(c, 0).start()
        own_copy(c, 1).start()

    def forward(c):
        own_copy(c, 0).wait_recv()
        forward_copy(c, 0).start()
        own_copy(c, 1).wait_recv()
        forward_copy(c, 1).start()

    def build_picks():
        for copy in code_copies:
            copy.wait_recv()
        for half, towards in ((0, along_z), (1, along_x)):
            for source in range(4):
                index = 0 if source == 0 else half * 3 + source
                for step in range(4):
                    code = codes[index, pl.ds(towards(step), 1), :]
                    picks[half, source, step * 64 : step * 64 + 64, :] = jnp.where(
                        code == slot_iota, 1.0, 0.0
                    ).astype(BF16)

    def pick_and_send(c):
        half = lax.rem(c, 2)
        forward_copy(c, 0).wait_recv()
        forward_copy(c, 1).wait_recv()
        mine = x * (1 - half) + z * half
        for source, delta in ((0, 0), (1, 3), (2, 1), (3, 2)):
            block = shifted[c] if source == 0 else line[c, source - 1]
            place = lax.rem(mine + delta, 4)
            picked = jnp.dot(picks[half, source], block, preferred_element_type=F32).astype(BF16)
            for step in range(1, 4):
                outgoing[c, step - 1, place] = picked[step * 64 : step * 64 + 64]
            rows[c, z * (1 - half) + place * half, place * (1 - half) + x * half] = picked[:64]
        for h in range(2):

            @pl.when(half == h)
            def _():
                for step in range(1, 4):
                    out_copy(c, step, h).start()

    def spread_probs():
        pre_load.wait()

        @pl.loop(1, 16)
        def _(step):
            tile_copy(step).wait_recv()

        mine = prob_tiles[:, pl.ds(me // 2, 1), :].reshape(16, 128)
        mine = jnp.where(lax.rem(me, 2) == 1, pltpu.roll(mine, 64, 1), mine)
        turned = jnp.concatenate([mine] * 8, axis=0).T
        for j in range(16):
            row_prob[j * 64 : j * 64 + 64, :] = jnp.broadcast_to(
                turned[:64, j : j + 1], (64, 128)
            )

        hidden_grad[...] = jnp.zeros_like(hidden_grad)

    def activate(first):
        @pl.loop(first, first + 2)
        def _(b):
            here = pl.ds(pl.multiple_of(b * 128, 128), 128)
            factor = row_prob[here, :]
            for q in range(8):
                gate = pre[here, q * 128 : q * 128 + 128].astype(F32)
                up = pre[here, 1024 + q * 128 : 1024 + q * 128 + 128].astype(F32)
                sig = jax.nn.sigmoid(gate)
                silu = gate * sig
                value = silu * up
                pre[here, q * 128 : q * 128 + 128] = (
                    up * sig * (1.0 + gate * (1.0 - sig))
                ).astype(BF16)
                pre[here, 1024 + q * 128 : 1024 + q * 128 + 128] = silu.astype(BF16)
                hidden[here, q * 128 : q * 128 + 128] = value.astype(BF16)
                scaled_t[q * 128 : q * 128 + 128, here] = (value * factor).T.astype(BF16)

    def arrived(c):
        for step in range(1, 4):
            out_copy(c, step, 0).wait_recv()

    def add_input_terms(c):
        weight_load(c).wait()

        hidden_grad[...] += lax.dot_general(
            rows[c].reshape(1024, COLS),
            weight[c],
            (((1,), (1,)), ((), ())),
            preferred_element_type=F32,
        )

    def weight_terms(c):
        there = pl.ds(pl.multiple_of(c * COLS, COLS), COLS)
        down_grad[:, there] = jnp.dot(
            scaled_t[...], rows[c].reshape(1024, COLS), preferred_element_type=F32
        ).astype(BF16)

    @pl.loop(0, chunks + LAG)
    def _(i):
        @pl.when(i < chunks)
        def _():
            send_own(i)

        @pl.when((i >= FORWARD_LAG) & (i < chunks + FORWARD_LAG))
        def _():
            forward(i - FORWARD_LAG)

        @pl.when(i == PICK_LAG - 1)
        def _():
            build_picks()

        @pl.when(i == 3)
        def _():
            spread_probs()

        @pl.when((i >= 4) & (i < 8))
        def _():
            activate(2 * i - 8)

        @pl.when((i >= PICK_LAG) & (i < chunks + PICK_LAG))
        def _():
            pick_and_send(i - PICK_LAG)

        @pl.when(i >= LAG)
        def _():
            arrived(i - LAG)
            add_input_terms(i - LAG)

            @pl.when(i < chunks + LAG - DEFERRED)
            def _():
                weight_terms(i - LAG)

    @pl.loop(0, 8)
    def _(b):
        here = pl.ds(pl.multiple_of(b * 128, 128), 128)
        factor = row_prob[here, :]
        total = jnp.zeros((128, 128), F32)
        for q in range(8):
            value = hidden_grad[here, q * 128 : q * 128 + 128]
            total = total + hidden[here, q * 128 : q * 128 + 128].astype(F32) * value
        back_tile[pl.ds(b, 1), :] = jnp.sum(total.T, axis=0, keepdims=True)

    def back_copy(step):
        return remote(
            back_tile,
            back_tiles.at[me],
            back_send.at[step],
            back_recv.at[step],
            (pipe, lax.rem(me + step, 16)),
        )

    @pl.loop(1, 16)
    def _(step):
        back_copy(step).start()

    back_tiles[me] = back_tile[...]
    @pl.loop(chunks - DEFERRED, chunks)
    def _(c):
        weight_terms(c)

    @pl.loop(0, 8)
    def _(b):
        here = pl.ds(pl.multiple_of(b * 128, 128), 128)
        factor = row_prob[here, :]
        for q in range(8):
            value = hidden_grad[here, q * 128 : q * 128 + 128] * factor
            for first in (q * 128, 1024 + q * 128):
                pre[here, first : first + 128] = (
                    value * pre[here, first : first + 128].astype(F32)
                ).astype(BF16)

    @pl.loop(1, 16)
    def _(step):
        back_copy(step).wait_recv()

    mine = back_tiles[:, pl.ds(me // 2, 1), :].reshape(16, 128)
    other = pltpu.roll(mine, 64, 1)
    low = lax.broadcasted_iota(jnp.int32, (16, 128), 1) < 64
    odd = lax.rem(me, 2) == 1
    back[...] = jnp.where(low == jnp.logical_not(odd), mine, other)

    for copy in code_copies:
        copy.wait_send()

    @pl.loop(1, 16)
    def _(step):
        tile_copy(step).wait_send()
        back_copy(step).wait_send()

    @pl.loop(0, chunks)
    def _(c):
        shift_copy(c).wait_send()
        for side in range(2):
            own_copy(c, side).wait_send()
            forward_copy(c, side).wait_send()
        for step in range(1, 4):
            out_copy(c, step, 0).wait_send()


def exchange(grad, route_t, prob_t, pre, weight):
    chunks = grad.shape[1] // COLS
    hbm = pl.BlockSpec(memory_space=pl.ANY)
    vmem = pl.BlockSpec(memory_space=pltpu.VMEM)
    dma = pltpu.SemaphoreType.DMA
    return pl.pallas_call(
        exchange_kernel,
        out_shape=(
            pltpu.VMEM((1024, 2048), BF16),
            pltpu.VMEM((1024, chunks * COLS), BF16),
            pltpu.VMEM((16, 128), F32),
            pltpu.VMEM((1024, 256), BF16),
            pltpu.VMEM((8, 256), jnp.int32),
        ),
        in_specs=[hbm] * 5,
        out_specs=(vmem,) * 5,
        scratch_shapes=[
            pltpu.VMEM((8, 256), BF16),
            pltpu.VMEM((1024, 1024), F32),
            pltpu.VMEM((chunks, 256, COLS), BF16),
            pltpu.VMEM((chunks, 3, 256, COLS), BF16),
            pltpu.VMEM((chunks, 3, 4, 64, COLS), BF16),
            pltpu.VMEM((chunks, 4, 4, 64, COLS), BF16),
            pltpu.VMEM((chunks, 1024, COLS), BF16),
            pltpu.VMEM((1024, 1024), BF16),
            pltpu.VMEM((1024, 1024), BF16),
            pltpu.VMEM((7, 16, 256), F32),
            pltpu.VMEM((2, 4, 256, 256), BF16),
            pltpu.VMEM((16, 8, 128), F32),
            pltpu.VMEM((8, 128), F32),
            pltpu.VMEM((16, 8, 128), F32),
            pltpu.VMEM((1024, 128), F32),
            dma((chunks + 3,)),
            dma((chunks,)),
            dma((chunks,)),
            dma((chunks, 2)),
            dma((chunks, 2)),
            dma((chunks, 4)),
            dma((chunks, 3)),
            dma((chunks, 3)),
            dma((6,)),
            dma((6,)),
            dma((16,)),
            dma((16,)),
            dma((16,)),
            dma((16,)),
        ],
        compiler_params=pltpu.CompilerParams(
            collective_id=0, has_side_effects=True, vmem_limit_bytes=50 * 2**20
        ),
        name="exchange",
    )(grad, route_t, prob_t, pre, weight)


def finish_kernel(
    preact_in, down_in, back, own_picks, routes, preact_out, down_out, prob_out, result_ref, sem
):
    copies = [
        pltpu.make_async_copy(down_in, down_out, sem.at[0]),
        pltpu.make_async_copy(preact_in, preact_out, sem.at[1]),
    ]
    for copy in copies:
        copy.start()
    diagonal = (
        lax.broadcasted_iota(jnp.int32, (16, 1024), 1) // 64
        == lax.broadcasted_iota(jnp.int32, (16, 1024), 0)
    )
    spread = jnp.where(diagonal, jnp.concatenate([back[...]] * 8, axis=1), 0.0)
    high = spread.astype(BF16)
    rest = spread - high.astype(F32)
    middle = rest.astype(BF16)
    small = (rest - middle.astype(F32)).astype(BF16)
    pieces = jnp.dot(
        jnp.concatenate([high, middle, small], axis=0), own_picks[...], preferred_element_type=F32
    )
    token_grad = pieces[:16] + pieces[16:32] + pieces[32:]
    result = jnp.zeros((8, 256), F32)
    for e in range(16):
        result = result + jnp.where(routes[...] == e, token_grad[e : e + 1, :], 0.0)
    result_ref[...] = result
    copies.append(pltpu.make_async_copy(result_ref, prob_out, sem.at[2]))
    copies[2].start()
    for copy in copies:
        copy.wait()


def finish(preact_grad, down_grad, back, own_picks, routes):
    shape = jax.ShapeDtypeStruct
    results = (preact_grad, down_grad, back, own_picks, routes)
    return pl.pallas_call(
        finish_kernel,
        out_shape=(
            shape(preact_grad.shape, BF16),
            shape(down_grad.shape, BF16),
            shape(routes.shape, F32),
        ),
        in_specs=[pl.BlockSpec(memory_space=pltpu.VMEM)] * 5,
        out_specs=(pl.BlockSpec(memory_space=pl.ANY),) * 3,
        scratch_shapes=[pltpu.VMEM(routes.shape, F32), pltpu.SemaphoreType.DMA((3,))],
        compiler_params=pltpu.CompilerParams(vmem_limit_bytes=2 * 2**20),
        name="finish",
    )(*(pltpu.with_memory_space_constraint(r, pltpu.VMEM) for r in results))


def on_device(boundary_grad, route_ids, route_probs, saved_preact, down_weight):
    preact_grad, down_grad, prob_grad = finish(
        *exchange(
            boundary_grad[0],
            route_ids[0].T,
            route_probs[0].T,
            saved_preact[0, 0],
            down_weight[0, 0],
        )
    )
    return (preact_grad[None, None], down_grad[None, None], prob_grad.T[None])


def solution(mesh):
    placed = (
        P("pipe", "expert", None),
        P("pipe", "expert", None),
        P("pipe", "expert", None),
        P("pipe", "expert", None, None),
        P("pipe", "expert", None, None),
    )
    return jax.shard_map(
        on_device,
        mesh=mesh,
        in_specs=placed,
        out_specs=(
            P("pipe", "expert", None, None),
            P("pipe", "expert", None, None),
            P("pipe", "expert", None),
        ),
        check_vma=False,
    )
```

```python
import functools

import jax
import jax.numpy as jnp
from jax import lax
from jax.experimental import pallas as pl
from jax.experimental.pallas import tpu as pltpu
from jax.sharding import PartitionSpec as P

MESH = pl.DeviceIdType.MESH
F32 = jnp.float32
BF16 = jnp.bfloat16
COLS = 256
SHIFTS = 4
FORWARD_LAG = 3
PICK_LAG = 6
LAG = 9
DEFERRED = 2


def exchange_kernel(
    grad_hbm,
    route_hbm,
    prob_hbm,
    pre_hbm,
    weight_hbm,
    pre,
    down_grad,
    back,
    own_picks,
    route_ref,
    prob_ref,
    hidden_grad,
    shifted,
    line,
    outgoing,
    rows,
    weight,
    hidden,
    scaled_t,
    codes,
    picks,
    prob_tiles,
    back_tile,
    back_tiles,
    row_prob,
    load_sem,
    shift_send,
    shift_recv,
    own_send,
    forward_send,
    line_recv,
    out_send,
    rows_recv,
    code_send,
    code_recv,
    tile_send,
    tile_recv,
    back_send,
    back_recv,
):
    chunks = shifted.shape[0]
    pipe = lax.axis_index("pipe")
    me = lax.axis_index("expert")
    z, x = me // 4, me % 4
    before = lax.rem(pipe + 7, 8)

    def along_x(step):
        return z * 4 + lax.rem(x + step, 4)

    def along_z(step):
        return lax.rem(z + step, 4) * 4 + x

    def first_axis(half, step):
        return along_x(step) * (1 - half) + along_z(step) * half

    def second_axis(half, step):
        return along_z(step) * (1 - half) + along_x(step) * half

    def remote(src, dst, send, recv, device):
        return pltpu.make_async_remote_copy(
            src_ref=src,
            dst_ref=dst,
            send_sem=send,
            recv_sem=recv,
            device_id=device,
            device_id_type=MESH,
        )

    barrier = pltpu.get_barrier_semaphore()
    for step in range(1, 16):
        pl.semaphore_signal(
            barrier, inc=1, device_id=(pipe, lax.rem(me + step, 16)), device_id_type=MESH
        )
    for step in (1, 7):
        pl.semaphore_signal(
            barrier, inc=1, device_id=(lax.rem(pipe + step, 8), me), device_id_type=MESH
        )

    small_loads = (
        pltpu.make_async_copy(route_hbm, route_ref, load_sem.at[chunks + 1]),
        pltpu.make_async_copy(prob_hbm, prob_ref, load_sem.at[chunks + 2]),
    )
    for load in small_loads:
        load.start()
    pre_load = pltpu.make_async_copy(pre_hbm, pre, load_sem.at[chunks])
    pre_load.start()

    def weight_load(c):
        return pltpu.make_async_copy(
            weight_hbm.at[:, pl.ds(pl.multiple_of(c * COLS, COLS), COLS)],
            weight.at[c],
            load_sem.at[c],
        )

    @pl.loop(0, chunks)
    def _(c):
        weight_load(c).start()

    pl.semaphore_wait(barrier, 17)

    def shift_copy(c):
        return remote(
            grad_hbm.at[:, pl.ds(pl.multiple_of(c * COLS, COLS), COLS)],
            shifted.at[c],
            shift_send.at[c],
            shift_recv.at[c],
            (before, me),
        )

    @pl.loop(0, SHIFTS)
    def _(c):
        shift_copy(c).start()

    for load in small_loads:
        load.wait()

    expert_iota = lax.broadcasted_iota(jnp.int32, (16, 256), 0)
    member = jnp.zeros((16, 256), F32)
    token_prob = jnp.zeros((16, 256), F32)
    for k in range(8):
        hit = route_ref[k : k + 1, :] == expert_iota
        member = member + jnp.where(hit, 1.0, 0.0)
        token_prob = token_prob + jnp.where(hit, prob_ref[k : k + 1, :].astype(F32), 0.0)
    earlier = (
        lax.broadcasted_iota(jnp.int32, (256, 256), 0)
        <= lax.broadcasted_iota(jnp.int32, (256, 256), 1)
    )
    rank = jnp.dot(
        member.astype(BF16), jnp.where(earlier, 1.0, 0.0).astype(BF16), preferred_element_type=F32
    )
    codes[0] = jnp.where(member > 0.5, rank - 1.0, -1.0)
    slot_iota = lax.broadcasted_iota(jnp.int32, (64, 256), 0).astype(F32)
    for e in range(16):
        own_picks[e * 64 : e * 64 + 64, :] = jnp.where(
            codes[0, e : e + 1, :] == slot_iota, 1.0, 0.0
        ).astype(BF16)
    diagonal = (
        lax.broadcasted_iota(jnp.int32, (16, 1024), 1) // 64
        == lax.broadcasted_iota(jnp.int32, (16, 1024), 0)
    )
    slot_probs = lax.dot_general(
        token_prob.astype(BF16),
        own_picks[...],
        (((1,), (1,)), ((), ())),
        preferred_element_type=F32,
    )
    slot_probs = jnp.sum(jnp.where(diagonal, slot_probs, 0.0), axis=0, keepdims=True)
    for r in range(8):
        prob_tiles[me, r : r + 1, :] = slot_probs[:, r * 128 : r * 128 + 128]

    code_copies = []
    for half, towards in ((0, along_x), (1, along_z)):
        for slot, step in ((1, 1), (2, 3), (3, 2)):
            index = half * 3 + slot
            code_copies.append(
                remote(
                    codes.at[0],
                    codes.at[index],
                    code_send.at[index - 1],
                    code_recv.at[index - 1],
                    (pipe, towards(step)),
                )
            )
    for copy in code_copies:
        copy.start()

    def tile_copy(step):
        return remote(
            prob_tiles.at[me],
            prob_tiles.at[me],
            tile_send.at[step],
            tile_recv.at[step],
            (pipe, lax.rem(me + step, 16)),
        )

    @pl.loop(1, 16)
    def _(step):
        tile_copy(step).start()

    def own_copy(c, side):
        half = lax.rem(c, 2)
        return remote(
            shifted.at[c],
            line.at[c, side],
            own_send.at[c, side],
            line_recv.at[c, side],
            (pipe, first_axis(half, 1 if side == 0 else 3)),
        )

    def forward_copy(c, side):
        half = lax.rem(c, 2)
        part = pl.ds(side * 128, 128)
        return remote(
            line.at[c, side, part],
            line.at[c, 2, part],
            forward_send.at[c, side],
            line_recv.at[c, 2 + side],
            (pipe, first_axis(half, 1 if side == 0 else 3)),
        )

    def out_copy(c, step, half):
        target = rows.at[c, z] if half == 0 else rows.at[c, :, x]
        return remote(
            outgoing.at[c, step - 1],
            target,
            out_send.at[c, step - 1],
            rows_recv.at[c, step - 1],
            (pipe, second_axis(half, step)),
        )

    def send_own(c):
        shift_copy(c).wait_recv()

        @pl.when(c + SHIFTS < chunks)
        def _():
            shift_copy(c + SHIFTS).start()

        own_copy(c, 0).start()
        own_copy(c, 1).start()

    def forward(c):
        own_copy(c, 0).wait_recv()
        forward_copy(c, 0).start()
        own_copy(c, 1).wait_recv()
        forward_copy(c, 1).start()

    def build_picks():
        for copy in code_copies:
            copy.wait_recv()
        for half, towards in ((0, along_z), (1, along_x)):
            for source in range(4):
                index = 0 if source == 0 else half * 3 + source
                for step in range(4):
                    code = codes[index, pl.ds(towards(step), 1), :]
                    picks[half, source, step * 64 : step * 64 + 64, :] = jnp.where(
                        code == slot_iota, 1.0, 0.0
                    ).astype(BF16)

    def pick_and_send(c):
        half = lax.rem(c, 2)
        forward_copy(c, 0).wait_recv()
        forward_copy(c, 1).wait_recv()
        mine = x * (1 - half) + z * half
        for source, delta in ((0, 0), (1, 3), (2, 1), (3, 2)):
            block = shifted[c] if source == 0 else line[c, source - 1]
            place = lax.rem(mine + delta, 4)
            picked = jnp.dot(picks[half, source], block, preferred_element_type=F32).astype(BF16)
            for step in range(1, 4):
                outgoing[c, step - 1, place] = picked[step * 64 : step * 64 + 64]
            rows[c, z * (1 - half) + place * half, place * (1 - half) + x * half] = picked[:64]
        for h in range(2):

            @pl.when(half == h)
            def _():
                for step in (2, 1, 3):
                    out_copy(c, step, h).start()

    def spread_probs():
        pre_load.wait()

        @pl.loop(1, 16)
        def _(step):
            tile_copy(step).wait_recv()

        mine = prob_tiles[:, pl.ds(me // 2, 1), :].reshape(16, 128)
        mine = jnp.where(lax.rem(me, 2) == 1, pltpu.roll(mine, 64, 1), mine)
        turned = jnp.concatenate([mine] * 8, axis=0).T
        for j in range(16):
            row_prob[j * 64 : j * 64 + 64, :] = jnp.broadcast_to(
                turned[:64, j : j + 1], (64, 128)
            )

        hidden_grad[...] = jnp.zeros_like(hidden_grad)

    def activate(first):
        @pl.loop(first, first + 2)
        def _(b):
            here = pl.ds(pl.multiple_of(b * 128, 128), 128)
            factor = row_prob[here, :]
            for q in range(8):
                gate = pre[here, q * 128 : q * 128 + 128].astype(F32)
                up = pre[here, 1024 + q * 128 : 1024 + q * 128 + 128].astype(F32)
                sig = jax.nn.sigmoid(gate)
                silu = gate * sig
                value = silu * up
                pre[here, q * 128 : q * 128 + 128] = (
                    up * sig * (1.0 + gate * (1.0 - sig))
                ).astype(BF16)
                pre[here, 1024 + q * 128 : 1024 + q * 128 + 128] = silu.astype(BF16)
                hidden[here, q * 128 : q * 128 + 128] = value.astype(BF16)
                scaled_t[q * 128 : q * 128 + 128, here] = (value * factor).T.astype(BF16)

    def arrived(c):
        for step in range(1, 4):
            out_copy(c, step, 0).wait_recv()

    def add_input_terms(c):
        weight_load(c).wait()

        hidden_grad[...] += lax.dot_general(
            rows[c].reshape(1024, COLS),
            weight[c],
            (((1,), (1,)), ((), ())),
            preferred_element_type=F32,
        )

    def weight_terms(c):
        there = pl.ds(pl.multiple_of(c * COLS, COLS), COLS)
        down_grad[:, there] = jnp.dot(
            scaled_t[...], rows[c].reshape(1024, COLS), preferred_element_type=F32
        ).astype(BF16)

    @pl.loop(0, chunks + LAG)
    def _(i):
        @pl.when(i < chunks)
        def _():
            send_own(i)

        @pl.when((i >= FORWARD_LAG) & (i < chunks + FORWARD_LAG))
        def _():
            forward(i - FORWARD_LAG)

        @pl.when(i == PICK_LAG - 1)
        def _():
            build_picks()

        @pl.when(i == 3)
        def _():
            spread_probs()

        @pl.when((i >= 4) & (i < 8))
        def _():
            activate(2 * i - 8)

        @pl.when((i >= PICK_LAG) & (i < chunks + PICK_LAG))
        def _():
            pick_and_send(i - PICK_LAG)

        @pl.when(i >= LAG)
        def _():
            arrived(i - LAG)
            add_input_terms(i - LAG)

            @pl.when(i < chunks + LAG - DEFERRED)
            def _():
                weight_terms(i - LAG)

    @pl.loop(0, 8)
    def _(b):
        here = pl.ds(pl.multiple_of(b * 128, 128), 128)
        factor = row_prob[here, :]
        total = jnp.zeros((128, 128), F32)
        for q in range(8):
            value = hidden_grad[here, q * 128 : q * 128 + 128]
            total = total + hidden[here, q * 128 : q * 128 + 128].astype(F32) * value
        back_tile[pl.ds(b, 1), :] = jnp.sum(total.T, axis=0, keepdims=True)

    def back_copy(step):
        return remote(
            back_tile,
            back_tiles.at[me],
            back_send.at[step],
            back_recv.at[step],
            (pipe, lax.rem(me + step, 16)),
        )

    @pl.loop(1, 16)
    def _(step):
        back_copy(step).start()

    back_tiles[me] = back_tile[...]
    @pl.loop(chunks - DEFERRED, chunks)
    def _(c):
        weight_terms(c)

    @pl.loop(0, 8)
    def _(b):
        here = pl.ds(pl.multiple_of(b * 128, 128), 128)
        factor = row_prob[here, :]
        for q in range(8):
            value = hidden_grad[here, q * 128 : q * 128 + 128] * factor
            for first in (q * 128, 1024 + q * 128):
                pre[here, first : first + 128] = (
                    value * pre[here, first : first + 128].astype(F32)
                ).astype(BF16)

    @pl.loop(1, 16)
    def _(step):
        back_copy(step).wait_recv()

    mine = back_tiles[:, pl.ds(me // 2, 1), :].reshape(16, 128)
    other = pltpu.roll(mine, 64, 1)
    low = lax.broadcasted_iota(jnp.int32, (16, 128), 1) < 64
    odd = lax.rem(me, 2) == 1
    back[...] = jnp.where(low == jnp.logical_not(odd), mine, other)

    for copy in code_copies:
        copy.wait_send()

    @pl.loop(1, 16)
    def _(step):
        tile_copy(step).wait_send()
        back_copy(step).wait_send()

    @pl.loop(0, chunks)
    def _(c):
        shift_copy(c).wait_send()
        for side in range(2):
            own_copy(c, side).wait_send()
            forward_copy(c, side).wait_send()
        for step in range(1, 4):
            out_copy(c, step, 0).wait_send()


def exchange(grad, route_t, prob_t, pre, weight):
    chunks = grad.shape[1] // COLS
    hbm = pl.BlockSpec(memory_space=pl.ANY)
    vmem = pl.BlockSpec(memory_space=pltpu.VMEM)
    dma = pltpu.SemaphoreType.DMA
    return pl.pallas_call(
        exchange_kernel,
        out_shape=(
            pltpu.VMEM((1024, 2048), BF16),
            pltpu.VMEM((1024, chunks * COLS), BF16),
            pltpu.VMEM((16, 128), F32),
            pltpu.VMEM((1024, 256), BF16),
            pltpu.VMEM((8, 256), jnp.int32),
        ),
        in_specs=[hbm] * 5,
        out_specs=(vmem,) * 5,
        scratch_shapes=[
            pltpu.VMEM((8, 256), BF16),
            pltpu.VMEM((1024, 1024), F32),
            pltpu.VMEM((chunks, 256, COLS), BF16),
            pltpu.VMEM((chunks, 3, 256, COLS), BF16),
            pltpu.VMEM((chunks, 3, 4, 64, COLS), BF16),
            pltpu.VMEM((chunks, 4, 4, 64, COLS), BF16),
            pltpu.VMEM((chunks, 1024, COLS), BF16),
            pltpu.VMEM((1024, 1024), BF16),
            pltpu.VMEM((1024, 1024), BF16),
            pltpu.VMEM((7, 16, 256), F32),
            pltpu.VMEM((2, 4, 256, 256), BF16),
            pltpu.VMEM((16, 8, 128), F32),
            pltpu.VMEM((8, 128), F32),
            pltpu.VMEM((16, 8, 128), F32),
            pltpu.VMEM((1024, 128), F32),
            dma((chunks + 3,)),
            dma((chunks,)),
            dma((chunks,)),
            dma((chunks, 2)),
            dma((chunks, 2)),
            dma((chunks, 4)),
            dma((chunks, 3)),
            dma((chunks, 3)),
            dma((6,)),
            dma((6,)),
            dma((16,)),
            dma((16,)),
            dma((16,)),
            dma((16,)),
        ],
        compiler_params=pltpu.CompilerParams(
            collective_id=0, has_side_effects=True, vmem_limit_bytes=50 * 2**20
        ),
        name="exchange",
    )(grad, route_t, prob_t, pre, weight)


def finish_kernel(
    preact_in, down_in, back, own_picks, routes, preact_out, down_out, prob_out, result_ref, sem
):
    copies = [
        pltpu.make_async_copy(down_in, down_out, sem.at[0]),
        pltpu.make_async_copy(preact_in, preact_out, sem.at[1]),
    ]
    for copy in copies:
        copy.start()
    diagonal = (
        lax.broadcasted_iota(jnp.int32, (16, 1024), 1) // 64
        == lax.broadcasted_iota(jnp.int32, (16, 1024), 0)
    )
    spread = jnp.where(diagonal, jnp.concatenate([back[...]] * 8, axis=1), 0.0)
    high = spread.astype(BF16)
    rest = spread - high.astype(F32)
    middle = rest.astype(BF16)
    small = (rest - middle.astype(F32)).astype(BF16)
    pieces = jnp.dot(
        jnp.concatenate([high, middle, small], axis=0), own_picks[...], preferred_element_type=F32
    )
    token_grad = pieces[:16] + pieces[16:32] + pieces[32:]
    result = jnp.zeros((8, 256), F32)
    for e in range(16):
        result = result + jnp.where(routes[...] == e, token_grad[e : e + 1, :], 0.0)
    result_ref[...] = result
    copies.append(pltpu.make_async_copy(result_ref, prob_out, sem.at[2]))
    copies[2].start()
    for copy in copies:
        copy.wait()


def finish(preact_grad, down_grad, back, own_picks, routes):
    shape = jax.ShapeDtypeStruct
    results = (preact_grad, down_grad, back, own_picks, routes)
    return pl.pallas_call(
        finish_kernel,
        out_shape=(
            shape(preact_grad.shape, BF16),
            shape(down_grad.shape, BF16),
            shape(routes.shape, F32),
        ),
        in_specs=[pl.BlockSpec(memory_space=pltpu.VMEM)] * 5,
        out_specs=(pl.BlockSpec(memory_space=pl.ANY),) * 3,
        scratch_shapes=[pltpu.VMEM(routes.shape, F32), pltpu.SemaphoreType.DMA((3,))],
        compiler_params=pltpu.CompilerParams(vmem_limit_bytes=2 * 2**20),
        name="finish",
    )(*(pltpu.with_memory_space_constraint(r, pltpu.VMEM) for r in results))


def on_device(boundary_grad, route_ids, route_probs, saved_preact, down_weight):
    preact_grad, down_grad, prob_grad = finish(
        *exchange(
            boundary_grad[0],
            route_ids[0].T,
            route_probs[0].T,
            saved_preact[0, 0],
            down_weight[0, 0],
        )
    )
    return (preact_grad[None, None], down_grad[None, None], prob_grad.T[None])


def solution(mesh):
    placed = (
        P("pipe", "expert", None),
        P("pipe", "expert", None),
        P("pipe", "expert", None),
        P("pipe", "expert", None, None),
        P("pipe", "expert", None, None),
    )
    return jax.shard_map(
        on_device,
        mesh=mesh,
        in_specs=placed,
        out_specs=(
            P("pipe", "expert", None, None),
            P("pipe", "expert", None, None),
            P("pipe", "expert", None),
        ),
        check_vma=False,
    )
```

```python
import functools

import jax
import jax.numpy as jnp
from jax import lax
from jax.experimental import pallas as pl
from jax.experimental.pallas import tpu as pltpu
from jax.sharding import PartitionSpec as P

MESH = pl.DeviceIdType.MESH
F32 = jnp.float32
BF16 = jnp.bfloat16
COLS = 256
SHIFTS = 4
FORWARD_LAG = 3
PICK_LAG = 6
LAG = 9
DEFERRED = 2


def exchange_kernel(
    grad_hbm,
    route_hbm,
    prob_hbm,
    pre_hbm,
    weight_hbm,
    pre,
    down_grad,
    back,
    own_picks,
    route_ref,
    prob_ref,
    hidden_grad,
    shifted,
    line,
    outgoing,
    rows,
    weight,
    hidden,
    scaled_t,
    codes,
    picks,
    prob_tiles,
    back_tile,
    back_tiles,
    row_prob,
    load_sem,
    shift_send,
    shift_recv,
    own_send,
    forward_send,
    line_recv,
    out_send,
    rows_recv,
    code_send,
    code_recv,
    tile_send,
    tile_recv,
    back_send,
    back_recv,
):
    chunks = shifted.shape[0]
    pipe = lax.axis_index("pipe")
    me = lax.axis_index("expert")
    z, x = me // 4, me % 4
    before = lax.rem(pipe + 7, 8)

    def along_x(step):
        return z * 4 + lax.rem(x + step, 4)

    def along_z(step):
        return lax.rem(z + step, 4) * 4 + x

    def first_axis(half, step):
        return along_x(step) * (1 - half) + along_z(step) * half

    def second_axis(half, step):
        return along_z(step) * (1 - half) + along_x(step) * half

    def remote(src, dst, send, recv, device):
        return pltpu.make_async_remote_copy(
            src_ref=src,
            dst_ref=dst,
            send_sem=send,
            recv_sem=recv,
            device_id=device,
            device_id_type=MESH,
        )

    barrier = pltpu.get_barrier_semaphore()
    for step in range(1, 16):
        pl.semaphore_signal(
            barrier, inc=1, device_id=(pipe, lax.rem(me + step, 16)), device_id_type=MESH
        )
    for step in (1, 7):
        pl.semaphore_signal(
            barrier, inc=1, device_id=(lax.rem(pipe + step, 8), me), device_id_type=MESH
        )

    small_loads = (
        pltpu.make_async_copy(route_hbm, route_ref, load_sem.at[chunks + 1]),
        pltpu.make_async_copy(prob_hbm, prob_ref, load_sem.at[chunks + 2]),
    )
    for load in small_loads:
        load.start()
    pre_load = pltpu.make_async_copy(pre_hbm, pre, load_sem.at[chunks])
    pre_load.start()

    def weight_load(c):
        return pltpu.make_async_copy(
            weight_hbm.at[:, pl.ds(pl.multiple_of(c * COLS, COLS), COLS)],
            weight.at[c],
            load_sem.at[c],
        )

    @pl.loop(0, chunks)
    def _(c):
        weight_load(c).start()

    pl.semaphore_wait(barrier, 17)

    def shift_copy(c):
        return remote(
            grad_hbm.at[:, pl.ds(pl.multiple_of(c * COLS, COLS), COLS)],
            shifted.at[c],
            shift_send.at[c],
            shift_recv.at[c],
            (before, me),
        )

    @pl.loop(0, SHIFTS)
    def _(c):
        shift_copy(c).start()

    for load in small_loads:
        load.wait()

    expert_iota = lax.broadcasted_iota(jnp.int32, (16, 256), 0)
    member = jnp.zeros((16, 256), F32)
    token_prob = jnp.zeros((16, 256), F32)
    for k in range(8):
        hit = route_ref[k : k + 1, :] == expert_iota
        member = member + jnp.where(hit, 1.0, 0.0)
        token_prob = token_prob + jnp.where(hit, prob_ref[k : k + 1, :].astype(F32), 0.0)
    earlier = (
        lax.broadcasted_iota(jnp.int32, (256, 256), 0)
        <= lax.broadcasted_iota(jnp.int32, (256, 256), 1)
    )
    rank = jnp.dot(
        member.astype(BF16), jnp.where(earlier, 1.0, 0.0).astype(BF16), preferred_element_type=F32
    )
    codes[0] = jnp.where(member > 0.5, rank - 1.0, -1.0)
    slot_iota = lax.broadcasted_iota(jnp.int32, (64, 256), 0).astype(F32)
    for e in range(16):
        own_picks[e * 64 : e * 64 + 64, :] = jnp.where(
            codes[0, e : e + 1, :] == slot_iota, 1.0, 0.0
        ).astype(BF16)
    diagonal = (
        lax.broadcasted_iota(jnp.int32, (16, 1024), 1) // 64
        == lax.broadcasted_iota(jnp.int32, (16, 1024), 0)
    )
    slot_probs = lax.dot_general(
        token_prob.astype(BF16),
        own_picks[...],
        (((1,), (1,)), ((), ())),
        preferred_element_type=F32,
    )
    slot_probs = jnp.sum(jnp.where(diagonal, slot_probs, 0.0), axis=0, keepdims=True)
    for r in range(8):
        prob_tiles[me, r : r + 1, :] = slot_probs[:, r * 128 : r * 128 + 128]

    code_copies = []
    for half, towards in ((0, along_x), (1, along_z)):
        for slot, step in ((1, 1), (2, 3), (3, 2)):
            index = half * 3 + slot
            code_copies.append(
                remote(
                    codes.at[0],
                    codes.at[index],
                    code_send.at[index - 1],
                    code_recv.at[index - 1],
                    (pipe, towards(step)),
                )
            )
    for copy in code_copies:
        copy.start()

    def tile_copy(step):
        return remote(
            prob_tiles.at[me],
            prob_tiles.at[me],
            tile_send.at[step],
            tile_recv.at[step],
            (pipe, lax.rem(me + step, 16)),
        )

    @pl.loop(1, 16)
    def _(step):
        tile_copy(step).start()

    def own_copy(c, side):
        half = lax.rem(c, 2)
        return remote(
            shifted.at[c],
            line.at[c, side],
            own_send.at[c, side],
            line_recv.at[c, side],
            (pipe, first_axis(half, 1 if side == 0 else 3)),
        )

    def forward_copy(c, side):
        half = lax.rem(c, 2)
        part = pl.ds(side * 128, 128)
        return remote(
            line.at[c, side, part],
            line.at[c, 2, part],
            forward_send.at[c, side],
            line_recv.at[c, 2 + side],
            (pipe, first_axis(half, 1 if side == 0 else 3)),
        )

    def out_copy(c, step, half):
        target = rows.at[c, z] if half == 0 else rows.at[c, :, x]
        return remote(
            outgoing.at[c, step - 1],
            target,
            out_send.at[c, step - 1],
            rows_recv.at[c, step - 1],
            (pipe, second_axis(half, step)),
        )

    def send_own(c):
        shift_copy(c).wait_recv()

        @pl.when(c + SHIFTS < chunks)
        def _():
            shift_copy(c + SHIFTS).start()

        own_copy(c, 0).start()
        own_copy(c, 1).start()

    def forward(c):
        own_copy(c, 0).wait_recv()
        forward_copy(c, 0).start()
        own_copy(c, 1).wait_recv()
        forward_copy(c, 1).start()

    def build_picks():
        for copy in code_copies:
            copy.wait_recv()
        for half, towards in ((0, along_z), (1, along_x)):
            for source in range(4):
                index = 0 if source == 0 else half * 3 + source
                for step in range(4):
                    code = codes[index, pl.ds(towards(step), 1), :]
                    picks[half, source, step * 64 : step * 64 + 64, :] = jnp.where(
                        code == slot_iota, 1.0, 0.0
                    ).astype(BF16)

    def pick_and_send(c):
        half = lax.rem(c, 2)
        forward_copy(c, 0).wait_recv()
        forward_copy(c, 1).wait_recv()
        mine = x * (1 - half) + z * half
        for source, delta in ((0, 0), (1, 3), (2, 1), (3, 2)):
            block = shifted[c] if source == 0 else line[c, source - 1]
            place = lax.rem(mine + delta, 4)
            picked = jnp.dot(picks[half, source], block, preferred_element_type=F32).astype(BF16)
            for step in range(1, 4):
                outgoing[c, step - 1, place] = picked[step * 64 : step * 64 + 64]
            rows[c, z * (1 - half) + place * half, place * (1 - half) + x * half] = picked[:64]
        for h in range(2):

            @pl.when(half == h)
            def _():
                for step in (2, 1, 3):
                    out_copy(c, step, h).start()

    def spread_probs():
        pre_load.wait()

        @pl.loop(1, 16)
        def _(step):
            tile_copy(step).wait_recv()

        mine = prob_tiles[:, pl.ds(me // 2, 1), :].reshape(16, 128)
        mine = jnp.where(lax.rem(me, 2) == 1, pltpu.roll(mine, 64, 1), mine)
        turned = jnp.concatenate([mine] * 8, axis=0).T
        for j in range(16):
            row_prob[j * 64 : j * 64 + 64, :] = jnp.broadcast_to(
                turned[:64, j : j + 1], (64, 128)
            )

        hidden_grad[...] = jnp.zeros_like(hidden_grad)

    def activate(first):
        @pl.loop(first, first + 2)
        def _(b):
            here = pl.ds(pl.multiple_of(b * 128, 128), 128)
            factor = row_prob[here, :]
            for q in range(8):
                gate = pre[here, q * 128 : q * 128 + 128].astype(F32)
                up = pre[here, 1024 + q * 128 : 1024 + q * 128 + 128].astype(F32)
                sig = jax.nn.sigmoid(gate)
                silu = gate * sig
                value = silu * up
                pre[here, q * 128 : q * 128 + 128] = (
                    up * sig * (1.0 + gate * (1.0 - sig))
                ).astype(BF16)
                pre[here, 1024 + q * 128 : 1024 + q * 128 + 128] = silu.astype(BF16)
                hidden[here, q * 128 : q * 128 + 128] = value.astype(BF16)
                scaled_t[q * 128 : q * 128 + 128, here] = (value * factor).T.astype(BF16)

    def arrived(c):
        for step in range(1, 4):
            out_copy(c, step, 0).wait_recv()

    def add_input_terms(c):
        weight_load(c).wait()

        hidden_grad[...] += lax.dot_general(
            rows[c].reshape(1024, COLS),
            weight[c],
            (((1,), (1,)), ((), ())),
            preferred_element_type=F32,
        )

    def weight_terms(c):
        there = pl.ds(pl.multiple_of(c * COLS, COLS), COLS)
        down_grad[:, there] = jnp.dot(
            scaled_t[...], rows[c].reshape(1024, COLS), preferred_element_type=F32
        ).astype(BF16)

    @pl.loop(0, chunks + LAG)
    def _(i):
        @pl.when((i >= FORWARD_LAG) & (i < chunks + FORWARD_LAG))
        def _():
            forward(i - FORWARD_LAG)

        @pl.when(i < chunks)
        def _():
            send_own(i)

        @pl.when(i == PICK_LAG - 1)
        def _():
            build_picks()

        @pl.when(i == 3)
        def _():
            spread_probs()

        @pl.when((i >= 4) & (i < 8))
        def _():
            activate(2 * i - 8)

        @pl.when((i >= PICK_LAG) & (i < chunks + PICK_LAG))
        def _():
            pick_and_send(i - PICK_LAG)

        @pl.when(i >= LAG)
        def _():
            arrived(i - LAG)
            add_input_terms(i - LAG)

            @pl.when(i < chunks + LAG - DEFERRED)
            def _():
                weight_terms(i - LAG)

    @pl.loop(0, 8)
    def _(b):
        here = pl.ds(pl.multiple_of(b * 128, 128), 128)
        factor = row_prob[here, :]
        total = jnp.zeros((128, 128), F32)
        for q in range(8):
            value = hidden_grad[here, q * 128 : q * 128 + 128]
            total = total + hidden[here, q * 128 : q * 128 + 128].astype(F32) * value
        back_tile[pl.ds(b, 1), :] = jnp.sum(total.T, axis=0, keepdims=True)

    def back_copy(step):
        return remote(
            back_tile,
            back_tiles.at[me],
            back_send.at[step],
            back_recv.at[step],
            (pipe, lax.rem(me + step, 16)),
        )

    @pl.loop(1, 16)
    def _(step):
        back_copy(step).start()

    back_tiles[me] = back_tile[...]
    @pl.loop(chunks - DEFERRED, chunks)
    def _(c):
        weight_terms(c)

    @pl.loop(0, 8)
    def _(b):
        here = pl.ds(pl.multiple_of(b * 128, 128), 128)
        factor = row_prob[here, :]
        for q in range(8):
            value = hidden_grad[here, q * 128 : q * 128 + 128] * factor
            for first in (q * 128, 1024 + q * 128):
                pre[here, first : first + 128] = (
                    value * pre[here, first : first + 128].astype(F32)
                ).astype(BF16)

    @pl.loop(1, 16)
    def _(step):
        back_copy(step).wait_recv()

    mine = back_tiles[:, pl.ds(me // 2, 1), :].reshape(16, 128)
    other = pltpu.roll(mine, 64, 1)
    low = lax.broadcasted_iota(jnp.int32, (16, 128), 1) < 64
    odd = lax.rem(me, 2) == 1
    back[...] = jnp.where(low == jnp.logical_not(odd), mine, other)

    for copy in code_copies:
        copy.wait_send()

    @pl.loop(1, 16)
    def _(step):
        tile_copy(step).wait_send()
        back_copy(step).wait_send()

    @pl.loop(0, chunks)
    def _(c):
        shift_copy(c).wait_send()
        for side in range(2):
            own_copy(c, side).wait_send()
            forward_copy(c, side).wait_send()
        for step in range(1, 4):
            out_copy(c, step, 0).wait_send()


def exchange(grad, route_t, prob_t, pre, weight):
    chunks = grad.shape[1] // COLS
    hbm = pl.BlockSpec(memory_space=pl.ANY)
    vmem = pl.BlockSpec(memory_space=pltpu.VMEM)
    dma = pltpu.SemaphoreType.DMA
    return pl.pallas_call(
        exchange_kernel,
        out_shape=(
            pltpu.VMEM((1024, 2048), BF16),
            pltpu.VMEM((1024, chunks * COLS), BF16),
            pltpu.VMEM((16, 128), F32),
            pltpu.VMEM((1024, 256), BF16),
            pltpu.VMEM((8, 256), jnp.int32),
        ),
        in_specs=[hbm] * 5,
        out_specs=(vmem,) * 5,
        scratch_shapes=[
            pltpu.VMEM((8, 256), BF16),
            pltpu.VMEM((1024, 1024), F32),
            pltpu.VMEM((chunks, 256, COLS), BF16),
            pltpu.VMEM((chunks, 3, 256, COLS), BF16),
            pltpu.VMEM((chunks, 3, 4, 64, COLS), BF16),
            pltpu.VMEM((chunks, 4, 4, 64, COLS), BF16),
            pltpu.VMEM((chunks, 1024, COLS), BF16),
            pltpu.VMEM((1024, 1024), BF16),
            pltpu.VMEM((1024, 1024), BF16),
            pltpu.VMEM((7, 16, 256), F32),
            pltpu.VMEM((2, 4, 256, 256), BF16),
            pltpu.VMEM((16, 8, 128), F32),
            pltpu.VMEM((8, 128), F32),
            pltpu.VMEM((16, 8, 128), F32),
            pltpu.VMEM((1024, 128), F32),
            dma((chunks + 3,)),
            dma((chunks,)),
            dma((chunks,)),
            dma((chunks, 2)),
            dma((chunks, 2)),
            dma((chunks, 4)),
            dma((chunks, 3)),
            dma((chunks, 3)),
            dma((6,)),
            dma((6,)),
            dma((16,)),
            dma((16,)),
            dma((16,)),
            dma((16,)),
        ],
        compiler_params=pltpu.CompilerParams(
            collective_id=0, has_side_effects=True, vmem_limit_bytes=50 * 2**20
        ),
        name="exchange",
    )(grad, route_t, prob_t, pre, weight)


def finish_kernel(
    preact_in, down_in, back, own_picks, routes, preact_out, down_out, prob_out, result_ref, sem
):
    copies = [
        pltpu.make_async_copy(down_in, down_out, sem.at[0]),
        pltpu.make_async_copy(preact_in, preact_out, sem.at[1]),
    ]
    for copy in copies:
        copy.start()
    diagonal = (
        lax.broadcasted_iota(jnp.int32, (16, 1024), 1) // 64
        == lax.broadcasted_iota(jnp.int32, (16, 1024), 0)
    )
    spread = jnp.where(diagonal, jnp.concatenate([back[...]] * 8, axis=1), 0.0)
    high = spread.astype(BF16)
    rest = spread - high.astype(F32)
    middle = rest.astype(BF16)
    small = (rest - middle.astype(F32)).astype(BF16)
    pieces = jnp.dot(
        jnp.concatenate([high, middle, small], axis=0), own_picks[...], preferred_element_type=F32
    )
    token_grad = pieces[:16] + pieces[16:32] + pieces[32:]
    result = jnp.zeros((8, 256), F32)
    for e in range(16):
        result = result + jnp.where(routes[...] == e, token_grad[e : e + 1, :], 0.0)
    result_ref[...] = result
    copies.append(pltpu.make_async_copy(result_ref, prob_out, sem.at[2]))
    copies[2].start()
    for copy in copies:
        copy.wait()


def finish(preact_grad, down_grad, back, own_picks, routes):
    shape = jax.ShapeDtypeStruct
    results = (preact_grad, down_grad, back, own_picks, routes)
    return pl.pallas_call(
        finish_kernel,
        out_shape=(
            shape(preact_grad.shape, BF16),
            shape(down_grad.shape, BF16),
            shape(routes.shape, F32),
        ),
        in_specs=[pl.BlockSpec(memory_space=pltpu.VMEM)] * 5,
        out_specs=(pl.BlockSpec(memory_space=pl.ANY),) * 3,
        scratch_shapes=[pltpu.VMEM(routes.shape, F32), pltpu.SemaphoreType.DMA((3,))],
        compiler_params=pltpu.CompilerParams(vmem_limit_bytes=2 * 2**20),
        name="finish",
    )(*(pltpu.with_memory_space_constraint(r, pltpu.VMEM) for r in results))


def on_device(boundary_grad, route_ids, route_probs, saved_preact, down_weight):
    preact_grad, down_grad, prob_grad = finish(
        *exchange(
            boundary_grad[0],
            route_ids[0].T,
            route_probs[0].T,
            saved_preact[0, 0],
            down_weight[0, 0],
        )
    )
    return (preact_grad[None, None], down_grad[None, None], prob_grad.T[None])


def solution(mesh):
    placed = (
        P("pipe", "expert", None),
        P("pipe", "expert", None),
        P("pipe", "expert", None),
        P("pipe", "expert", None, None),
        P("pipe", "expert", None, None),
    )
    return jax.shard_map(
        on_device,
        mesh=mesh,
        in_specs=placed,
        out_specs=(
            P("pipe", "expert", None, None),
            P("pipe", "expert", None, None),
            P("pipe", "expert", None),
        ),
        check_vma=False,
    )
```
